256 devices in a mesh: chan: 64 (over y, x_lo, z), rep: 4 (over x_hi, core).
Axes of the slice: x: 4 (x_hi: 2, x_lo: 2; x = x_hi * 2 + x_lo), y: 4, z: 8, core: 2. Of those that a mesh axis runs over, the one named last changes fastest.
Arguments:
- records: bfloat16 [2, 64, 256, 2048], P(None, None, 'rep', 'chan'), may hold values from -6 to 6
- sources: int32 [128], replicated, may hold values from 0 to 16383
- dead_list: int32 [2, 1024], replicated, may hold values from 0 to 16383
Outputs:
- correlations: float32 [128, 64, 16384], P('rep', None, 'chan')
The draws below stay inside these ranges and needn't reach their ends.
All inputs are finite; a program needn't handle non-finite values.
Results may differ from the reference program's by a relative error of at most 0.0072.
Values may be sent and summed in bfloat16 or wider, within the bound.
A program may use at most 64 MiB of HBM per device.

```python
import math
import jax
import jax.numpy as jnp
from jax import lax

STACK_WINDOWS = 2
WINDOW_SAMPLES = 2048
K = 256
K0 = 16
HALF = 32
WH = 32
LAGS = 64
SRC = 128
CHANNELS_PER_BLK = 256
CH = 16384
NDEAD = 1024
N_CHAN = 64
N_REP = 4


def plant(drawn, key, smallest, high):
    dims = drawn.shape
    spot = [jax.random.randint(jax.random.fold_in(key, axis), (), 0, dims[axis]) for axis in range(len(dims))]
    drawn = drawn.at[tuple(spot)].set(smallest)
    longest = dims.index(max(dims))
    spot[longest] = (spot[longest] + 1) % dims[longest]
    return drawn.at[tuple(spot)].set(high)


def shard_levels(stream_key, dims, pieces, least, high):
    loudness, own = 1.0, jax.random.fold_in(stream_key, 6)
    for dim, blocks in pieces:
        draws = jnp.exp(jax.random.uniform(jax.random.fold_in(own, dim), (blocks,), jnp.float32, least / len(pieces), high / len(pieces)))
        loudness = loudness * jnp.repeat(draws, dims[dim] // blocks).reshape([-1 if axis == dim else 1 for axis in range(len(dims))])
    return loudness


def gaussian(stream_key, extent, deviation, most, shards=(), kind=jnp.bfloat16):
    factor_of = shard_levels(stream_key, extent, shards, -0.22, 0.18) if shards else 1.0
    values = jax.random.normal(stream_key, extent, jnp.float32) * deviation * factor_of
    return jnp.minimum(jnp.maximum(values, -most), most).astype(kind)


def setup_inputs(seed: int = 0) -> dict:
    splits = jax.random.split(jax.random.key(seed), 4)
    records = gaussian(splits[0], (STACK_WINDOWS, N_CHAN, CHANNELS_PER_BLK, WINDOW_SAMPLES), 1.0, 6.0, ((2, 4), (3, 64)))
    sources = plant(jax.random.randint(splits[1], (SRC,), 0, CH), jax.random.fold_in(splits[1], 1), 0, CH - 1).astype(jnp.int32)
    dead_list = plant(jax.random.randint(splits[2], (STACK_WINDOWS, NDEAD), 0, CH), jax.random.fold_in(splits[2], 1), 0, CH - 1).astype(jnp.int32)
    return dict(records=records, sources=sources, dead_list=dead_list)


tile_span = 128
tiny_eps = 1e-06

def live_table(dead_list, total):
    window_count, listed = dead_list.shape
    window_rows = jnp.broadcast_to(jnp.arange(window_count, dtype=jnp.int32)[:, None], (window_count, listed))
    return jnp.ones((window_count, total), jnp.float32).at[window_rows, dead_list].set(0.0)

def running_mean(records):
    length = records.shape[-1]
    blocks = length // tile_span
    leading = records.shape[:-1]
    magnitude = jnp.abs(records)
    padded = jnp.pad(magnitude, [(0, 0)] * (records.ndim - 1) + [(tile_span, tile_span)])
    before = padded[..., :length].reshape(leading + (blocks, tile_span))
    middle = magnitude.reshape(leading + (blocks, tile_span))
    after = padded[..., 2 * tile_span:].reshape(leading + (blocks, tile_span))
    views = jnp.concatenate([before, middle, after], axis=-1).reshape(-1, 3 * tile_span)
    offsets = jnp.arange(3 * tile_span, dtype=jnp.int32)[:, None] - tile_span
    targets = jnp.arange(tile_span, dtype=jnp.int32)[None, :]
    band_unit_mask = (jnp.abs(offsets - targets) <= HALF).astype(jnp.bfloat16)
    totals = jnp.dot(views, band_unit_mask, preferred_element_type=jnp.float32).reshape(leading + (length,))
    sample = jnp.arange(length, dtype=jnp.int32)
    counts = (jnp.minimum(sample, HALF) + jnp.minimum(length - 1 - sample, HALF) + 1).astype(jnp.float32)
    return totals / counts

def dft_table(length):
    sample = jnp.arange(length, dtype=jnp.int32)[:, None]
    bin_index = K0 + jnp.arange(K, dtype=jnp.int32)[None, :]
    phase = sample * bin_index % length
    angle = phase.astype(jnp.float32) * (2.0 * math.pi / length)
    return jnp.concatenate([jnp.cos(angle), -jnp.sin(angle)], axis=1).astype(jnp.bfloat16)

def whiten(spectrum):
    real_part = spectrum[:, :K]
    imag_part = spectrum[:, K:]
    amplitude = jnp.sqrt(real_part * real_part + imag_part * imag_part)
    index_row = jnp.arange(K, dtype=jnp.int32)[:, None]
    index_col = jnp.arange(K, dtype=jnp.int32)[None, :]
    band = (jnp.abs(index_row - index_col) <= WH).astype(jnp.float32)
    smoothed_amplitude = jnp.dot(amplitude, band, precision=lax.Precision.HIGHEST) / lax.optimization_barrier(jnp.sum(band, axis=0))
    return (spectrum / (jnp.concatenate([smoothed_amplitude, smoothed_amplitude], axis=1) + tiny_eps)).astype(jnp.bfloat16)

def preprocess(records):
    mean_abs = running_mean(records)
    normed = (records.astype(jnp.float32) / (mean_abs + tiny_eps)).astype(jnp.bfloat16)
    spectrum = jnp.dot(normed, dft_table(records.shape[-1]), preferred_element_type=jnp.float32)
    return whiten(spectrum)

def lag_kernel(source_spectrum):
    bin_index = K0 + jnp.arange(K, dtype=jnp.int32)[None, :]
    lag_index = jnp.arange(LAGS, dtype=jnp.int32)[:, None] - LAGS // 2
    phase = jnp.mod(lag_index * bin_index, WINDOW_SAMPLES)
    angle = phase.astype(jnp.float32) * (2.0 * math.pi / WINDOW_SAMPLES)
    cosine_lookup = jnp.cos(angle)[None, :, None, :]
    sin_table = jnp.sin(angle)[None, :, None, :]
    real_part = source_spectrum[:, None, :, :K].astype(jnp.float32)
    imag_part = source_spectrum[:, None, :, K:].astype(jnp.float32)
    with_real = real_part * cosine_lookup + imag_part * sin_table
    with_imag = imag_part * cosine_lookup - real_part * sin_table
    return jnp.concatenate([with_real, with_imag], axis=3).astype(jnp.bfloat16)

def correlate(kernel, spectra_wide, source_live, chan_live):
    summed = lax.dot_general(kernel.astype(jnp.float32), spectra_wide, (((2, 3), (0, 2)), ((), ())), precision=lax.Precision.HIGHEST)
    pairs = jnp.dot(source_live.T, chan_live, precision=lax.Precision.HIGHEST)
    return summed / (math.sqrt(K) * jnp.maximum(pairs, 1.0))[:, None, :]

def reference(records, sources, dead_list):
    window_count, groups, group_share, length = records.shape
    total = groups * group_share
    live = live_table(dead_list, total)
    flat = records.reshape(window_count, total, length)
    masked = jnp.where(live[:, :, None] > 0.5, flat, jnp.zeros_like(flat))
    spectra = lax.map(preprocess, masked.reshape(-1, group_share, length)).reshape(window_count, total, 2 * K)
    source_spectrum = jnp.transpose(spectra[:, sources, :], (1, 0, 2))
    source_live = live[:, sources]
    quarter = SRC // N_REP
    spectra_wide = spectra.astype(jnp.float32)

    def one_block(block):
        return correlate(lag_kernel(block[0]), spectra_wide, block[1], live)
    blocks = (source_spectrum.reshape(N_REP, quarter, window_count, 2 * K), jnp.transpose(source_live.reshape(window_count, N_REP, quarter), (1, 0, 2)))
    result = lax.map(one_block, blocks)
    return result.reshape(SRC, LAGS, total)
```

```python
import functools
import math

import jax
import jax.numpy as jnp
import numpy as np
from jax import lax
from jax.experimental import pallas as pl
from jax.experimental.pallas import tpu as pltpu
from jax.sharding import PartitionSpec as P

WINDOW_SAMPLES = 2048
K = 256
K0 = 16
HALF = 32
WH = 32
LAGS = 64
EPS = 1e-06
Z = 8

MESH = pl.DeviceIdType.MESH
BF16 = jnp.bfloat16
F32 = jnp.float32


def tables(length):
    m = ((K0 + np.arange(K))[:, None] * np.arange(length)[None, :]) % length
    angle = m.astype(np.float64) * (2.0 * math.pi / length)
    dft = np.concatenate([np.cos(angle), -np.sin(angle)], axis=0).astype(jnp.bfloat16)
    row, col = np.arange(128)[:, None], np.arange(256)[None, :]
    band = (np.abs(col - 64 - row) <= HALF).astype(jnp.bfloat16)
    j = np.arange(K)
    smooth = (np.abs(j[:, None] - j[None, :]) <= WH).astype(np.float32)
    count = np.broadcast_to(1.0 / smooth.sum(axis=1, keepdims=True), (K, 128)).astype(np.float32)
    tau = np.arange(LAGS)[:, None] - LAGS // 2
    phi = ((tau * (K0 + j)[None, :]) % length).astype(np.float64) * (2.0 * math.pi / length)
    lag = np.stack([np.cos(phi), np.sin(phi)]).astype(np.float32)
    return dft, band, smooth.astype(jnp.bfloat16), count, lag


def lane_iota(shape):
    return lax.broadcasted_iota(jnp.int32, shape, len(shape) - 1)


def whiten(load_rows, dft, band, smooth, count, absbuf, normed):
    length = normed.shape[0]
    blocks = length // 128
    zero = jnp.zeros((64, 128), BF16)
    absbuf[0:64, :] = zero
    absbuf[64 + length :, :] = zero

    def fill(b, carry):
        absbuf[pl.ds(pl.multiple_of(64 + b * 128, 64), 128), :] = jnp.abs(load_rows(b))
        return carry

    lax.fori_loop(0, blocks, fill, 0)

    def norm(b, carry):
        start = pl.multiple_of(b * 128, 128)
        total = jnp.dot(band[...], absbuf[pl.ds(start, 256), :], preferred_element_type=F32)
        t = lax.broadcasted_iota(jnp.int32, (128, 128), 0) + b * 128
        n = (jnp.minimum(t, HALF) + jnp.minimum(length - 1 - t, HALF) + 1).astype(F32)
        x = load_rows(b).astype(F32)
        normed[pl.ds(start, 128), :] = (x * n / (total + EPS * n)).astype(BF16)
        return carry

    lax.fori_loop(0, blocks, norm, 0)
    spectrum = jnp.dot(dft[...], normed[...], preferred_element_type=F32)
    re, im = spectrum[:K], spectrum[K:]
    amp = jnp.sqrt(re * re + im * im)
    high = amp.astype(BF16)
    rest = amp - high.astype(F32)
    mid = rest.astype(BF16)
    low = (rest - mid.astype(F32)).astype(BF16)
    s = smooth[...]
    total = (
        jnp.dot(s, low, preferred_element_type=F32)
        + jnp.dot(s, mid, preferred_element_type=F32)
        + jnp.dot(s, high, preferred_element_type=F32)
    )
    scale = 1.0 / (total * count[...] + EPS)
    return re * scale, im * scale


def gather_kernel(
    chans, reps,
    rec_hbm, src_ref, dead_ref, dft_hbm, band, smooth, count, lag,
    rhs_out, lk_out, inv_out,
    rec, dft, packed, recv, picks, pickrecv, srcbuf, own, gath, absbuf, normed, srcspec, livesrc,
    sem_in, sem_dft, a_send, a_recv, p_send, p_recv, z_send, z_recv, y_send, y_recv, g_send, g_recv,
):
    c, r = lax.axis_index("chan"), lax.axis_index("rep")
    z, yx = lax.rem(c, Z), c // Z
    nyx = chans // Z
    barrier = pltpu.get_barrier_semaphore()

    load = pltpu.make_async_copy(rec_hbm, rec, sem_in)
    load.start()
    load_dft = pltpu.make_async_copy(dft_hbm, dft, sem_dft)
    load_dft.start()

    def greet(k, carry):
        pl.semaphore_signal(barrier, inc=1, device_id={"chan": lax.rem(c + k, chans), "rep": r}, device_id_type=MESH)
        return carry

    lax.fori_loop(1, chans, greet, 0)
    for k in range(1, reps):
        pl.semaphore_signal(barrier, inc=1, device_id={"chan": c, "rep": lax.rem(r + k, reps)}, device_id_type=MESH)

    load.wait()

    def pack(g, carry):
        packed[g] = jnp.concatenate([rec[0, g], rec[1, g]], axis=1)
        return carry

    lax.fori_loop(0, chans, pack, 0)
    recv[c] = packed[c]
    pl.semaphore_wait(barrier, chans - 1 + reps - 1)

    def send(k, carry):
        d = lax.rem(c + k, chans)
        pltpu.make_async_remote_copy(
            packed.at[d], recv.at[c], a_send, a_recv, device_id={"chan": d, "rep": r}, device_id_type=MESH
        ).start()
        return carry

    lax.fori_loop(1, chans, send, 0)

    src = src_ref[...]
    within = src & 255
    mine = jnp.where((within >> 6) == r, within & 63, -1)
    row = lax.broadcasted_iota(jnp.int32, (128, 128), 0)
    sel = jnp.concatenate(
        [(row == mine).astype(BF16), (row - 64 == jnp.where(mine < 0, -1000, mine)).astype(BF16)], axis=1
    )
    block = src >> 8
    block2 = jnp.concatenate([block, block], axis=1)

    def pick(g, acc):
        part = jnp.dot(packed[g], sel, preferred_element_type=F32)
        return acc + jnp.where(block2 == g, part, 0.0)

    acc = lax.fori_loop(0, chans, pick, jnp.zeros((32, 256), F32))
    lane = lane_iota((32, 128))
    for q in range(reps):
        first = pltpu.roll(acc[:, :128], (128 - 32 * q) % 128, 1)
        second = pltpu.roll(acc[:, 128:], (32 - 32 * q) % 128, 1)
        picks[q] = jnp.where(lane < 32, first, second).astype(BF16)
    pickrecv[r] = picks[r]
    for k in range(1, reps):
        d = lax.rem(r + k, reps)
        pltpu.make_async_remote_copy(
            picks.at[d], pickrecv.at[r], p_send.at[k], p_recv.at[k], device_id={"chan": c, "rep": d}, device_id_type=MESH
        ).start()

    dead = dead_ref[...]
    eye = lax.broadcasted_iota(jnp.int32, (128, 128), 0) == lane_iota((128, 128))
    src_col = jnp.sum(jnp.where(eye, jnp.broadcast_to(src, (128, 128)), 0), axis=1, keepdims=True)
    ones = jnp.ones((8, 1024), BF16)
    chan_live = []
    for w in range(2):
        listed = dead[w : w + 1, :]
        hit = jnp.sum((listed == src_col).astype(F32), axis=1, keepdims=True)
        livesrc[w] = jnp.broadcast_to(jnp.where(hit > 0.5, 0.0, 1.0), (128, 128))
        here = jnp.where((listed >> 8) == c, listed & 255, -1)
        rows = lax.broadcasted_iota(jnp.int32, (256, 1024), 0)
        onehot = (rows == here).astype(BF16)
        hits = lax.dot_general(ones, onehot, (((1,), (1,)), ((), ())), preferred_element_type=F32)
        chan_live.append(jnp.where(hits[0:1] > 0.5, 0.0, 1.0))
    start = pl.multiple_of(r * 32, 32)
    ls = [livesrc[w, pl.ds(start, 32), :] for w in range(2)]
    pairs = jnp.concatenate(
        [
            ls[0] * chan_live[0][:, h * 128 : h * 128 + 128] + ls[1] * chan_live[1][:, h * 128 : h * 128 + 128]
            for h in range(2)
        ],
        axis=1,
    )
    inv_out[...] = 1.0 / (math.sqrt(K) * jnp.maximum(pairs, 1.0))

    for k in range(1, reps):
        d = lax.rem(r + k, reps)
        cp = pltpu.make_async_remote_copy(
            picks.at[d], pickrecv.at[r], p_send.at[k], p_recv.at[k], device_id={"chan": c, "rep": d}, device_id_type=MESH
        )
        cp.wait_send()
        cp.wait_recv()
    total = pickrecv[0].astype(F32)
    for q in range(1, reps):
        total = total + pickrecv[q].astype(F32)
    half = jnp.where(lane[:16] < 64, total[:16], pltpu.roll(total[16:], 64, 1))
    srcbuf[c] = half.astype(BF16)

    def z_copy(k):
        return pltpu.make_async_remote_copy(
            srcbuf.at[c], srcbuf.at[c], z_send, z_recv,
            device_id={"chan": yx * Z + lax.rem(z + k, Z), "rep": r}, device_id_type=MESH,
        )

    def z_start(k, carry):
        z_copy(k).start()
        return carry

    lax.fori_loop(1, Z, z_start, 0)
    some = srcbuf.at[pl.ds(0, Z - 1)]
    bulk = pltpu.make_async_remote_copy(
        some, some, z_send, z_recv, device_id={"chan": c, "rep": lax.rem(r + 1, reps)}, device_id_type=MESH
    )
    bulk.wait_send()
    bulk.wait_recv()

    def y_start(k, carry):
        span = srcbuf.at[pl.ds(yx * Z, Z)]
        pltpu.make_async_remote_copy(
            span, span, y_send, y_recv,
            device_id={"chan": lax.rem(yx + k, nyx) * Z + z, "rep": r}, device_id_type=MESH,
        ).start()
        return carry

    lax.fori_loop(1, nyx, y_start, 0)
    some = srcbuf.at[pl.ds(0, (nyx - 1) * Z)]
    bulk = pltpu.make_async_remote_copy(
        some, some, y_send, y_recv, device_id={"chan": c, "rep": lax.rem(r + 1, reps)}, device_id_type=MESH
    )
    bulk.wait_send()
    bulk.wait_recv()

    load_dft.wait()

    def source_rows(b):
        parts = []
        for i in range(4):
            piece = srcbuf[b * 4 + i]
            parts += [piece, pltpu.roll(piece.astype(F32), 64, 1).astype(BF16)]
        return jnp.concatenate(parts, axis=0)

    re, im = whiten(source_rows, dft, band, smooth, count, absbuf, normed)
    ls_col = jnp.concatenate([ls[0], ls[1]], axis=0)[:, :1]
    for part, value in enumerate((re, im)):
        rows = jnp.transpose(value)[:64] * ls_col
        srcspec[part] = rows.astype(BF16).astype(F32)

    def lag_rows(s, carry):
        at = pl.multiple_of(s * LAGS, LAGS)
        for w in range(2):
            u = srcspec[0, pl.ds(w * 32 + s, 1), :]
            v = srcspec[1, pl.ds(w * 32 + s, 1), :]
            cos, sin = lag[0], lag[1]
            lk_out[pl.ds(at, LAGS), w * 512 : w * 512 + 256] = (u * cos + v * sin).astype(BF16)
            lk_out[pl.ds(at, LAGS), w * 512 + 256 : w * 512 + 512] = (v * cos - u * sin).astype(BF16)
        return carry

    lax.fori_loop(0, 32, lag_rows, 0)

    some = recv.at[pl.ds(0, chans - 1)]
    bulk = pltpu.make_async_remote_copy(
        packed.at[pl.ds(0, chans - 1)], some, a_send, a_recv,
        device_id={"chan": c, "rep": lax.rem(r + 1, reps)}, device_id_type=MESH,
    )
    bulk.wait_send()
    bulk.wait_recv()

    def own_rows(b):
        return jnp.concatenate([recv[b * 4 + i] for i in range(4)], axis=0)

    re, im = whiten(own_rows, dft, band, smooth, count, absbuf, normed)
    halves = []
    for w in range(2):
        quarter = jnp.zeros((1, 128), F32)
        for q in range(reps):
            tile = chan_live[w][:, (q // 2) * 128 : (q // 2) * 128 + 128]
            quarter = jnp.where(r == q, pltpu.roll(tile, (64 * (w - q)) % 128, 1), quarter)
        halves.append(quarter)
    mask = jnp.where(lane_iota((1, 128)) < 64, halves[0], halves[1])
    own[0:K, :] = (re * mask).astype(BF16)
    own[K:, :] = (im * mask).astype(BF16)
    gath[r] = own[...]

    def g_copy(k):
        return pltpu.make_async_remote_copy(
            own, gath.at[r], g_send.at[k], g_recv.at[k],
            device_id={"chan": c, "rep": lax.rem(r + k, reps)}, device_id_type=MESH,
        )

    for k in range(1, reps):
        g_copy(k).start()
    for k in range(1, reps):
        cp = g_copy(k)
        cp.wait_send()
        cp.wait_recv()
    low = lane_iota((512, 128)) < 64
    for h in range(2):
        a, b = gath[2 * h].astype(F32), gath[2 * h + 1].astype(F32)
        rhs_out[0:512, h * 128 : h * 128 + 128] = jnp.where(low, a, pltpu.roll(b, 64, 1)).astype(BF16)
        rhs_out[512:1024, h * 128 : h * 128 + 128] = jnp.where(low, pltpu.roll(a, 64, 1), b).astype(BF16)


def correlate_kernel(lk, rhs, inv, out):
    step = pl.program_id(0)
    summed = jnp.dot(lk[...], rhs[...], preferred_element_type=F32)
    for i in range(out.shape[0]):
        out[i] = summed[i * LAGS : (i + 1) * LAGS] * inv[pl.ds(step * out.shape[0] + i, 1), :]


def solution(mesh):
    chans, reps = mesh.shape["chan"], mesh.shape["rep"]

    def shards(records, sources, dead_list):
        windows, groups, width, span = records.shape
        length = span * chans
        dft, band, smooth, count, lag = tables(length)
        quarter = sources.shape[0] // reps
        vmem = pl.BlockSpec(memory_space=pltpu.VMEM)
        anyspace = pl.BlockSpec(memory_space=pl.ANY)
        dma = pltpu.SemaphoreType.DMA
        rhs, lk, inv = pl.pallas_call(
            functools.partial(gather_kernel, chans, reps),
            out_shape=[
                jax.ShapeDtypeStruct((1024, 256), BF16),
                jax.ShapeDtypeStruct((quarter * LAGS, 1024), BF16),
                jax.ShapeDtypeStruct((quarter, 256), F32),
            ],
            in_specs=[anyspace, vmem, vmem, anyspace, vmem, vmem, vmem, vmem],
            out_specs=[vmem] * 3,
            scratch_shapes=[
                pltpu.VMEM((windows, groups, span, width), BF16),
                pltpu.VMEM((512, length), BF16),
                pltpu.VMEM((chans, span, 128), BF16),
                pltpu.VMEM((chans, span, 128), BF16),
                pltpu.VMEM((reps, span, 128), BF16),
                pltpu.VMEM((reps, span, 128), BF16),
                pltpu.VMEM((chans, 16, 128), BF16),
                pltpu.VMEM((512, 128), BF16),
                pltpu.VMEM((reps, 512, 128), BF16),
                pltpu.VMEM((length + 128, 128), BF16),
                pltpu.VMEM((length, 128), BF16),
                pltpu.VMEM((2, 64, 256), F32),
                pltpu.VMEM((2, 128, 128), F32),
                dma, dma, dma, dma, dma((reps,)), dma((reps,)), dma, dma, dma, dma, dma((reps,)), dma((reps,)),
            ],
            compiler_params=pltpu.CompilerParams(
                collective_id=0, has_side_effects=True, vmem_limit_bytes=48 << 20
            ),
            name="gather_spectra",
        )(
            jnp.transpose(records, (0, 1, 3, 2)),
            sources.reshape(1, -1),
            dead_list,
            jnp.asarray(dft),
            jnp.asarray(band),
            jnp.asarray(smooth),
            jnp.asarray(count),
            jnp.asarray(lag),
        )
        step = 4
        return pl.pallas_call(
            correlate_kernel,
            grid=(quarter // step,),
            out_shape=jax.ShapeDtypeStruct((quarter, LAGS, 256), F32),
            in_specs=[
                pl.BlockSpec((step * LAGS, 1024), lambda i: (i, 0)),
                pl.BlockSpec((1024, 256), lambda i: (0, 0)),
                pl.BlockSpec((quarter, 256), lambda i: (0, 0)),
            ],
            out_specs=pl.BlockSpec((step, LAGS, 256), lambda i: (i, 0, 0)),
            name="correlate",
        )(lk, rhs, inv)

    return jax.shard_map(
        shards,
        mesh=mesh,
        in_specs=(P(None, None, "rep", "chan"), P(), P()),
        out_specs=P("rep", None, "chan"),
        check_vma=False,
    )
```

```python
import functools
import math

import jax
import jax.numpy as jnp
import numpy as np
from jax import lax
from jax.experimental import pallas as pl
from jax.experimental.pallas import tpu as pltpu
from jax.sharding import PartitionSpec as P

K = 256
K0 = 16
HALF = 32
WH = 32
LAGS = 64
EPS = 1e-06
Z = 8

MESH = pl.DeviceIdType.MESH
BF16 = jnp.bfloat16
F32 = jnp.float32


def tables(length):
    m = ((K0 + np.arange(K))[:, None] * np.arange(length)[None, :]) % length
    angle = m.astype(np.float64) * (2.0 * math.pi / length)
    dft = np.concatenate([np.cos(angle), -np.sin(angle)], axis=0).astype(jnp.bfloat16)
    tau = np.arange(LAGS)[:, None] - LAGS // 2
    phi = ((tau * (K0 + np.arange(K))[None, :]) % length).astype(np.float64) * (2.0 * math.pi / length)
    lag = np.stack([np.cos(phi), np.sin(phi)]).astype(np.float32)
    return dft, lag


def iota(shape, axis):
    return lax.broadcasted_iota(jnp.int32, shape, axis)


def swap(x):
    return pltpu.roll(x, 64, 1)


def whiten(buf, dft, absbuf, xbuf, normed):
    blocks = buf.shape[0]
    top = blocks * 16
    low = iota((16, 128), 1) < 64

    def spread(b, carry):
        for i in range(8):
            at = b * 8 + i
            first, second = buf[at], buf[at + blocks // 2]
            x0 = jnp.where(low, first, swap(second))
            x1 = jnp.where(low, swap(first), second)
            rows = pl.multiple_of(at * 32, 32)
            xbuf[pl.ds(rows, 16), :] = x0
            xbuf[pl.ds(rows + 16, 16), :] = x1
            absbuf[pl.ds(rows + 64, 16), :] = jnp.abs(x0)
            absbuf[pl.ds(rows + 80, 16), :] = jnp.abs(x1)
        return carry

    lax.fori_loop(0, blocks // 16, spread, 0)
    low = iota((64, 128), 1) < 64
    zero = jnp.zeros((64, 128), BF16)
    absbuf[0:64, :] = jnp.where(low, zero, swap(absbuf[top : top + 64, :]))
    absbuf[top + 64 :, :] = jnp.where(low, swap(absbuf[64:128, :]), zero)
    band = (jnp.abs(iota((128, 256), 1) - 64 - iota((128, 256), 0)) <= HALF).astype(BF16)

    for b in range(top // 128):
        start = b * 128
        total = jnp.dot(band, absbuf[pl.ds(start, 256), :], preferred_element_type=F32)
        t = iota((128, 128), 0) + b * 128 + jnp.where(iota((128, 128), 1) < 64, 0, top)
        n = (jnp.minimum(t, HALF) + jnp.minimum(2 * top - 1 - t, HALF) + 1).astype(F32)
        x = xbuf[pl.ds(start, 128), :].astype(F32)
        normed[pl.ds(start, 128), :] = (x * n / (total + EPS * n)).astype(BF16)
    x = normed[...]
    spectrum = jnp.dot(dft[:, :top], x, preferred_element_type=F32)
    other = jnp.dot(dft[:, top:], x, preferred_element_type=F32)
    spectrum = spectrum + pltpu.roll(other, 64, 1)
    re, im = spectrum[:K], spectrum[K:]
    amp = jnp.sqrt(re * re + im * im)
    high = amp.astype(BF16)
    rest = amp - high.astype(F32)
    mid = rest.astype(BF16)
    near = (jnp.abs(iota((K, K), 0) - iota((K, K), 1)) <= WH).astype(BF16)
    total = jnp.dot(near, mid, preferred_element_type=F32) + jnp.dot(near, high, preferred_element_type=F32)
    j = iota((K, 128), 0)
    n = (jnp.minimum(j, WH) + jnp.minimum(K - 1 - j, WH) + 1).astype(F32)
    scale = 1.0 / (total / n + EPS)
    return re * scale, im * scale


def gather_kernel(
    chans, reps,
    rec_hbm, src_hbm, dead_hbm, dft_hbm, lag_hbm,
    out,
    rec, src_ref, dead_ref, dft, lag,
    packed, recv, cols, picks, pickrecv, srcbuf, gath, rhs, lk, inv, absbuf, xbuf, normed, srcspec, livesrc,
    sem_in, a_send, a_recv, p_send, p_recv, z_send, z_recv, y_send, y_recv, g_send, g_recv,
):
    c, r = lax.axis_index("chan"), lax.axis_index("rep")
    z, yx = lax.rem(c, Z), c // Z
    nyx = chans // Z
    barrier = pltpu.get_barrier_semaphore()

    loads = [
        pltpu.make_async_copy(a, b, sem_in.at[i])
        for i, (a, b) in enumerate(
            [(rec_hbm, rec), (src_hbm, src_ref), (dead_hbm, dead_ref), (dft_hbm, dft), (lag_hbm, lag)]
        )
    ]
    for load in loads:
        load.start()

    def greet(k, carry):
        pl.semaphore_signal(barrier, inc=1, device_id={"chan": lax.rem(c + k, chans), "rep": r}, device_id_type=MESH)
        return carry

    lax.fori_loop(1, chans, greet, 0)
    for k in range(1, reps):
        pl.semaphore_signal(barrier, inc=1, device_id={"chan": c, "rep": lax.rem(r + k, reps)}, device_id_type=MESH)

    loads[0].wait()

    def pack(i, carry):
        for k in range(8):
            g = i * 8 + k
            for w in range(2):
                packed[w, g] = jnp.concatenate([rec[w, g, 0:16], rec[w, g, 16:32]], axis=1)
        return carry

    lax.fori_loop(0, chans // 8, pack, 0)
    for w in range(2):
        recv[w, c] = packed[w, c]

    pl.semaphore_wait(barrier, chans - 1 + reps - 1)

    def send_part(w, first, last):
        def send(k, carry):
            d = lax.rem(c + k, chans)
            pltpu.make_async_remote_copy(
                packed.at[w, d], recv.at[w, c], a_send.at[w], a_recv.at[w],
                device_id={"chan": d, "rep": r}, device_id_type=MESH,
            ).start()
            return carry

        lax.fori_loop(first, last, send, 0)

    send_part(0, 1, chans)

    loads[1].wait()
    src = src_ref[...]
    within = src & 255
    mine = jnp.where((within >> 6) == r, within & 63, -1000)
    row = iota((128, 128), 0)
    sel = jnp.concatenate([(row == mine).astype(BF16), (row - 64 == mine).astype(BF16)], axis=1)
    block = src >> 8
    block2 = jnp.concatenate([block, block], axis=1)
    accs = []
    for w in range(2):
        cols[...] = jnp.dot(packed[w].reshape(chans * 16, 128), sel, preferred_element_type=F32)

        def pick(i, acc):
            for k in range(8):
                g = i * 8 + k
                part = cols[pl.ds(pl.multiple_of(g * 16, 16), 16), :]
                acc = acc + jnp.where(block2 == g, part, 0.0)
            return acc

        accs.append(lax.fori_loop(0, chans // 8, pick, jnp.zeros((16, 256), F32)))
    lane = iota((16, 128), 1)
    for q in range(reps):
        value = jnp.zeros((16, 128), F32)
        for th in range(2):
            for w in range(2):
                to = th * 64 + w * 32
                piece = pltpu.roll(accs[w][:, th * 128 : th * 128 + 128], (to - 32 * q) % 128, 1)
                value = jnp.where((lane >= to) & (lane < to + 32), piece, value)
        picks[q] = value.astype(BF16)
    pickrecv[r] = picks[r]

    def p_copy(k):
        d = lax.rem(r + k, reps)
        return pltpu.make_async_remote_copy(
            picks.at[d], pickrecv.at[r], p_send.at[k], p_recv.at[k], device_id={"chan": c, "rep": d}, device_id_type=MESH
        )

    for k in range(1, reps):
        p_copy(k).start()

    loads[2].wait()
    dead = dead_ref[...]
    eye = iota((128, 128), 0) == iota((128, 128), 1)
    src_col = jnp.sum(jnp.where(eye, jnp.broadcast_to(src, (128, 128)), 0), axis=1, keepdims=True)
    ones = jnp.ones((8, 1024), BF16)
    chan_live = []
    for w in range(2):
        listed = dead[w : w + 1, :]
        hit = jnp.sum((listed == src_col).astype(F32), axis=1, keepdims=True)
        livesrc[w] = jnp.broadcast_to(jnp.where(hit > 0.5, 0.0, 1.0), (128, 128))
        here = jnp.where((listed >> 8) == c, listed & 255, -1)
        onehot = (iota((256, 1024), 0) == here).astype(BF16)
        hits = lax.dot_general(ones, onehot, (((1,), (1,)), ((), ())), preferred_element_type=F32)
        chan_live.append(jnp.where(hits[0:1] > 0.5, 0.0, 1.0))
    start = pl.multiple_of(r * 32, 32)
    ls = [livesrc[w, pl.ds(start, 32), :] for w in range(2)]
    for h in range(2):
        span = slice(h * 128, h * 128 + 128)
        pairs = ls[0] * chan_live[0][:, span] + ls[1] * chan_live[1][:, span]
        inv[:, span] = 1.0 / (math.sqrt(K) * jnp.maximum(pairs, 1.0))

    for k in range(1, reps):
        p_copy(k).wait_send()
        p_copy(k).wait_recv()
    total = pickrecv[0].astype(F32)
    for q in range(1, reps):
        total = total + pickrecv[q].astype(F32)
    srcbuf[c] = total.astype(BF16)

    def z_start(k, carry):
        pltpu.make_async_remote_copy(
            srcbuf.at[c], srcbuf.at[c], z_send, z_recv,
            device_id={"chan": yx * Z + lax.rem(z + k, Z), "rep": r}, device_id_type=MESH,
        ).start()
        return carry

    def y_start(k, carry):
        span = srcbuf.at[pl.ds(yx * Z, Z)]
        pltpu.make_async_remote_copy(
            span, span, y_send, y_recv,
            device_id={"chan": lax.rem(yx + k, nyx) * Z + z, "rep": r}, device_id_type=MESH,
        ).start()
        return carry

    def wait_all(some, send, recv):
        bulk = pltpu.make_async_remote_copy(
            some, some, send, recv, device_id={"chan": c, "rep": lax.rem(r + 1, reps)}, device_id_type=MESH
        )
        bulk.wait_send()
        bulk.wait_recv()

    lax.fori_loop(1, Z, z_start, 0)
    send_part(1, 1, chans)
    wait_all(srcbuf.at[pl.ds(0, Z - 1)], z_send, z_recv)
    lax.fori_loop(1, nyx, y_start, 0)
    loads[3].wait()
    loads[4].wait()
    def lag_rows(s, carry):
        at = pl.multiple_of(s * LAGS, LAGS)
        for w in range(2):
            u = srcspec[0, pl.ds(w * 32 + s, 1), :]
            v = srcspec[1, pl.ds(w * 32 + s, 1), :]
            cos, sin = lag[0], lag[1]
            lk[w, pl.ds(at, LAGS), 0:256] = (u * cos + v * sin).astype(BF16)
            lk[w, pl.ds(at, LAGS), 256:512] = (v * cos - u * sin).astype(BF16)
        return carry

    near, far = jnp.bitwise_xor(r, 1), jnp.bitwise_xor(r, 2)

    def g_copy(w, k):
        slot = far if k == 2 else r
        return pltpu.make_async_remote_copy(
            gath.at[w, slot], gath.at[w, slot], g_send.at[w, k], g_recv.at[w, k],
            device_id={"chan": c, "rep": far if k == 1 else near}, device_id_type=MESH,
        )

    def own_part(w):
        wait_all(recv.at[w, pl.ds(0, chans - 1)], a_send.at[w], a_recv.at[w])
        re, im = whiten(recv.at[w], dft, absbuf, xbuf, normed)
        mask = jnp.zeros((1, 128), F32)
        for q in range(reps):
            tile = chan_live[w][:, (q // 2) * 128 : (q // 2) * 128 + 128]
            mask = jnp.where(r == q, pltpu.roll(tile, (64 * q) % 128, 1), mask)
        re, im = re * mask, im * mask
        gath[w, r] = jnp.where(iota((K, 128), 1) < 64, re, pltpu.roll(im, 64, 1)).astype(BF16)
        g_copy(w, 1).start()
        g_copy(w, 0).start()

    def forward(w):
        g_copy(w, 1).wait_recv()
        g_copy(w, 2).start()

    def correlate(w):
        g_copy(w, 0).wait_recv()
        g_copy(w, 2).wait_recv()
        for k in range(3):
            g_copy(w, k).wait_send()
        low = iota((K, 128), 1) < 64
        for h in range(2):
            a, b = gath[w, 2 * h], gath[w, 2 * h + 1]
            rhs[0:K, h * 128 : h * 128 + 128] = jnp.where(low, a, swap(b))
            rhs[K:, h * 128 : h * 128 + 128] = jnp.where(low, swap(a), b)

        def rows(i, carry):
            at = pl.multiple_of(i * 256, 256)
            part = jnp.dot(lk[w, pl.ds(at, 256), :], rhs[...], preferred_element_type=F32)
            for k in range(4):
                piece = part[k * LAGS : (k + 1) * LAGS]
                if w == 0:
                    out[i * 4 + k] = piece
                else:
                    out[i * 4 + k] = (out[i * 4 + k] + piece) * inv[pl.ds(i * 4 + k, 1), :]
            return carry

        lax.fori_loop(0, lk.shape[1] // 256, rows, 0)

    own_part(0)
    wait_all(srcbuf.at[pl.ds(0, (nyx - 1) * Z)], y_send, y_recv)
    re, im = whiten(srcbuf, dft, absbuf, xbuf, normed)
    ls_col = jnp.concatenate([ls[0], ls[1]], axis=0)[:, :1]
    for part, value in enumerate((re, im)):
        rows = jnp.transpose(value)[:64] * ls_col
        srcspec[part] = rows.astype(BF16).astype(F32)

    lax.fori_loop(0, 32, lag_rows, 0)

    forward(0)
    own_part(1)
    correlate(0)
    forward(1)
    correlate(1)


def solution(mesh):
    chans, reps = mesh.shape["chan"], mesh.shape["rep"]

    def shards(records, sources, dead_list):
        windows, groups, width, span = records.shape
        length = span * chans
        dft, lag = tables(length)
        quarter = sources.shape[0] // reps
        vmem = pl.BlockSpec(memory_space=pltpu.VMEM)
        hbm = pl.BlockSpec(memory_space=pltpu.HBM)
        dma = pltpu.SemaphoreType.DMA
        return pl.pallas_call(
            functools.partial(gather_kernel, chans, reps),
            out_shape=jax.ShapeDtypeStruct((quarter, LAGS, 256), F32),
            in_specs=[hbm] * 5,
            out_specs=vmem,
            scratch_shapes=[
                pltpu.VMEM((windows, groups, span, width), BF16),
                pltpu.VMEM((1, sources.shape[0]), jnp.int32),
                pltpu.VMEM(dead_list.shape, jnp.int32),
                pltpu.VMEM((512, length), BF16),
                pltpu.VMEM((2, LAGS, K), F32),
                pltpu.VMEM((2, chans, 16, 128), BF16),
                pltpu.VMEM((2, chans, 16, 128), BF16),
                pltpu.VMEM((chans * 16, 256), F32),
                pltpu.VMEM((reps, 16, 128), BF16),
                pltpu.VMEM((reps, 16, 128), BF16),
                pltpu.VMEM((chans, 16, 128), BF16),
                pltpu.VMEM((2, reps, K, 128), BF16),
                pltpu.VMEM((2 * K, 256), BF16),
                pltpu.VMEM((2, quarter * LAGS, 2 * K), BF16),
                pltpu.VMEM((quarter, 256), F32),
                pltpu.VMEM((length // 2 + 128, 128), BF16),
                pltpu.VMEM((length // 2, 128), BF16),
                pltpu.VMEM((length // 2, 128), BF16),
                pltpu.VMEM((2, 64, 256), F32),
                pltpu.VMEM((2, 128, 128), F32),
                dma((5,)), dma((2,)), dma((2,)), dma((reps,)), dma((reps,)),
                dma, dma, dma, dma, dma((2, 3)), dma((2, 3)),
            ],
            compiler_params=pltpu.CompilerParams(
                collective_id=0, has_side_effects=True, vmem_limit_bytes=48 << 20
            ),
            name="correlations",
        )(
            *[
                pltpu.with_memory_space_constraint(x, pltpu.HBM)
                for x in (
                    jnp.transpose(records, (0, 1, 3, 2)),
                    sources.reshape(1, -1),
                    dead_list,
                    jnp.asarray(dft),
                    jnp.asarray(lag),
                )
            ]
        )

    return jax.shard_map(
        shards,
        mesh=mesh,
        in_specs=(P(None, None, "rep", "chan"), P(), P()),
        out_specs=P("rep", None, "chan"),
        check_vma=False,
    )
```

```python
import functools
import math

import jax
import jax.numpy as jnp
import numpy as np
from jax import lax
from jax.experimental import pallas as pl
from jax.experimental.pallas import tpu as pltpu
from jax.sharding import PartitionSpec as P

K = 256
K0 = 16
HALF = 32
WH = 32
LAGS = 64
EPS = 1e-06
Z = 8

MESH = pl.DeviceIdType.MESH
BF16 = jnp.bfloat16
F32 = jnp.float32


def tables(length):
    m = ((K0 + np.arange(K))[:, None] * np.arange(length)[None, :]) % length
    angle = m.astype(np.float64) * (2.0 * math.pi / length)
    dft = np.concatenate([np.cos(angle), -np.sin(angle)], axis=0).astype(jnp.bfloat16)
    tau = np.arange(LAGS)[:, None] - LAGS // 2
    phi = ((tau * (K0 + np.arange(K))[None, :]) % length).astype(np.float64) * (2.0 * math.pi / length)
    lag = np.stack([np.cos(phi), np.sin(phi)]).astype(np.float32)
    return dft, lag


def iota(shape, axis):
    return lax.broadcasted_iota(jnp.int32, shape, axis)


def swap(x):
    return pltpu.roll(x, 64, 1)


def whiten(buf, dft, absbuf, xbuf, normed):
    blocks = buf.shape[0]
    top = blocks * 16
    low = iota((16, 128), 1) < 64

    def spread(b, carry):
        for i in range(8):
            at = b * 8 + i
            first, second = buf[at], buf[at + blocks // 2]
            x0 = jnp.where(low, first, swap(second))
            x1 = jnp.where(low, swap(first), second)
            rows = pl.multiple_of(at * 32, 32)
            xbuf[pl.ds(rows, 16), :] = x0
            xbuf[pl.ds(rows + 16, 16), :] = x1
            absbuf[pl.ds(rows + 64, 16), :] = jnp.abs(x0)
            absbuf[pl.ds(rows + 80, 16), :] = jnp.abs(x1)
        return carry

    lax.fori_loop(0, blocks // 16, spread, 0)
    low = iota((64, 128), 1) < 64
    zero = jnp.zeros((64, 128), BF16)
    absbuf[0:64, :] = jnp.where(low, zero, swap(absbuf[top : top + 64, :]))
    absbuf[top + 64 :, :] = jnp.where(low, swap(absbuf[64:128, :]), zero)
    band = (jnp.abs(iota((128, 256), 1) - 64 - iota((128, 256), 0)) <= HALF).astype(BF16)

    for b in range(top // 128):
        start = b * 128
        total = jnp.dot(band, absbuf[pl.ds(start, 256), :], preferred_element_type=F32)
        t = iota((128, 128), 0) + b * 128 + jnp.where(iota((128, 128), 1) < 64, 0, top)
        n = (jnp.minimum(t, HALF) + jnp.minimum(2 * top - 1 - t, HALF) + 1).astype(F32)
        x = xbuf[pl.ds(start, 128), :].astype(F32)
        normed[pl.ds(start, 128), :] = (x * n / (total + EPS * n)).astype(BF16)
    x = normed[...]
    spectrum = jnp.dot(dft[:, :top], x, preferred_element_type=F32)
    other = jnp.dot(dft[:, top:], x, preferred_element_type=F32)
    spectrum = spectrum + pltpu.roll(other, 64, 1)
    re, im = spectrum[:K], spectrum[K:]
    amp = jnp.sqrt(re * re + im * im)
    high = amp.astype(BF16)
    rest = amp - high.astype(F32)
    mid = rest.astype(BF16)
    near = (jnp.abs(iota((K, K), 0) - iota((K, K), 1)) <= WH).astype(BF16)
    total = jnp.dot(near, mid, preferred_element_type=F32) + jnp.dot(near, high, preferred_element_type=F32)
    j = iota((K, 128), 0)
    n = (jnp.minimum(j, WH) + jnp.minimum(K - 1 - j, WH) + 1).astype(F32)
    scale = 1.0 / (total / n + EPS)
    return re * scale, im * scale


def gather_kernel(
    chans, reps,
    rec_hbm, src_hbm, dead_hbm, dft_hbm, lag_hbm,
    out,
    rec, src_ref, dead_ref, dft, lag,
    packed, recv, cols, picks, pickrecv, srcbuf, gath, rhs, lk, inv, absbuf, xbuf, normed, srcspec, livesrc,
    sem_in, a_send, a_recv, p_send, p_recv, z_send, z_recv, y_send, y_recv, g_send, g_recv,
):
    c, r = lax.axis_index("chan"), lax.axis_index("rep")
    z, yx = lax.rem(c, Z), c // Z
    nyx = chans // Z
    barrier = pltpu.get_barrier_semaphore()

    loads = [
        pltpu.make_async_copy(a, b, sem_in.at[i])
        for i, (a, b) in enumerate(
            [
                (rec_hbm.at[0], rec.at[0]), (src_hbm, src_ref), (dead_hbm, dead_ref), (dft_hbm, dft), (lag_hbm, lag),
                (rec_hbm.at[1], rec.at[1]),
            ]
        )
    ]
    for i in (0, 5, 1, 2, 3, 4):
        loads[i].start()

    def greet(k, carry):
        pl.semaphore_signal(barrier, inc=1, device_id={"chan": lax.rem(c + k, chans), "rep": r}, device_id_type=MESH)
        return carry

    lax.fori_loop(1, chans, greet, 0)
    for k in range(1, reps):
        pl.semaphore_signal(barrier, inc=1, device_id={"chan": c, "rep": lax.rem(r + k, reps)}, device_id_type=MESH)

    loads[0].wait()

    def pack_window(w):
        def pack(i, carry):
            for k in range(8):
                g = i * 8 + k
                packed[w, g] = jnp.concatenate([rec[w, g, 0:16], rec[w, g, 16:32]], axis=1)
            return carry

        lax.fori_loop(0, chans // 8, pack, 0)
        recv[w, c] = packed[w, c]

    pack_window(0)
    pl.semaphore_wait(barrier, chans - 1 + reps - 1)

    some_zero, some_one = chans * 3 // 8, chans * 5 // 8

    def send_part(w, first, last):
        def send(k, carry):
            d = lax.rem(c + k, chans)
            pltpu.make_async_remote_copy(
                packed.at[w, d], recv.at[w, c], a_send.at[w], a_recv.at[w],
                device_id={"chan": d, "rep": r}, device_id_type=MESH,
            ).start()
            return carry

        lax.fori_loop(first, last, send, 0)

    send_part(0, 1, some_zero)
    loads[5].wait()
    pack_window(1)

    loads[1].wait()
    src = src_ref[...]
    within = src & 255
    mine = jnp.where((within >> 6) == r, within & 63, -1000)
    row = iota((128, 128), 0)
    sel = jnp.concatenate([(row == mine).astype(BF16), (row - 64 == mine).astype(BF16)], axis=1)
    block = src >> 8
    block2 = jnp.concatenate([block, block], axis=1)
    accs = []
    for w in range(2):
        cols[...] = jnp.dot(packed[w].reshape(chans * 16, 128), sel, preferred_element_type=F32)

        def pick(i, acc):
            for k in range(8):
                g = i * 8 + k
                part = cols[pl.ds(pl.multiple_of(g * 16, 16), 16), :]
                acc = acc + jnp.where(block2 == g, part, 0.0)
            return acc

        accs.append(lax.fori_loop(0, chans // 8, pick, jnp.zeros((16, 256), F32)))
    lane = iota((16, 128), 1)
    for q in range(reps):
        value = jnp.zeros((16, 128), F32)
        for th in range(2):
            for w in range(2):
                to = th * 64 + w * 32
                piece = pltpu.roll(accs[w][:, th * 128 : th * 128 + 128], (to - 32 * q) % 128, 1)
                value = jnp.where((lane >= to) & (lane < to + 32), piece, value)
        picks[q] = value.astype(BF16)
    pickrecv[r] = picks[r]

    def p_copy(k):
        d = lax.rem(r + k, reps)
        return pltpu.make_async_remote_copy(
            picks.at[d], pickrecv.at[r], p_send.at[k], p_recv.at[k], device_id={"chan": c, "rep": d}, device_id_type=MESH
        )

    for k in range(1, reps):
        p_copy(k).start()
    send_part(0, some_zero, chans)

    loads[2].wait()
    dead = dead_ref[...]
    eye = iota((128, 128), 0) == iota((128, 128), 1)
    src_col = jnp.sum(jnp.where(eye, jnp.broadcast_to(src, (128, 128)), 0), axis=1, keepdims=True)
    ones = jnp.ones((8, 1024), BF16)
    chan_live = []
    for w in range(2):
        listed = dead[w : w + 1, :]
        hit = jnp.sum((listed == src_col).astype(F32), axis=1, keepdims=True)
        livesrc[w] = jnp.broadcast_to(jnp.where(hit > 0.5, 0.0, 1.0), (128, 128))
        here = jnp.where((listed >> 8) == c, listed & 255, -1)
        onehot = (iota((256, 1024), 0) == here).astype(BF16)
        hits = lax.dot_general(ones, onehot, (((1,), (1,)), ((), ())), preferred_element_type=F32)
        chan_live.append(jnp.where(hits[0:1] > 0.5, 0.0, 1.0))
    start = pl.multiple_of(r * 32, 32)
    ls = [livesrc[w, pl.ds(start, 32), :] for w in range(2)]
    for h in range(2):
        span = slice(h * 128, h * 128 + 128)
        pairs = ls[0] * chan_live[0][:, span] + ls[1] * chan_live[1][:, span]
        inv[:, span] = 1.0 / (math.sqrt(K) * jnp.maximum(pairs, 1.0))

    for k in range(1, reps):
        p_copy(k).wait_send()
        p_copy(k).wait_recv()
    total = pickrecv[0].astype(F32)
    for q in range(1, reps):
        total = total + pickrecv[q].astype(F32)
    srcbuf[c] = total.astype(BF16)

    def z_start(k, carry):
        pltpu.make_async_remote_copy(
            srcbuf.at[c], srcbuf.at[c], z_send, z_recv,
            device_id={"chan": yx * Z + lax.rem(z + k, Z), "rep": r}, device_id_type=MESH,
        ).start()
        return carry

    def y_start(k, carry):
        span = srcbuf.at[pl.ds(yx * Z, Z)]
        pltpu.make_async_remote_copy(
            span, span, y_send, y_recv,
            device_id={"chan": lax.rem(yx + k, nyx) * Z + z, "rep": r}, device_id_type=MESH,
        ).start()
        return carry

    def wait_all(some, send, recv):
        bulk = pltpu.make_async_remote_copy(
            some, some, send, recv, device_id={"chan": c, "rep": lax.rem(r + 1, reps)}, device_id_type=MESH
        )
        bulk.wait_send()
        bulk.wait_recv()

    lax.fori_loop(1, Z, z_start, 0)
    send_part(1, 1, some_one)
    wait_all(srcbuf.at[pl.ds(0, Z - 1)], z_send, z_recv)
    lax.fori_loop(1, nyx, y_start, 0)
    send_part(1, some_one, chans)
    loads[3].wait()
    loads[4].wait()
    def lag_rows(s, carry):
        at = pl.multiple_of(s * LAGS, LAGS)
        for w in range(2):
            u = srcspec[0, pl.ds(w * 32 + s, 1), :]
            v = srcspec[1, pl.ds(w * 32 + s, 1), :]
            cos, sin = lag[0], lag[1]
            lk[w, pl.ds(at, LAGS), 0:256] = (u * cos + v * sin).astype(BF16)
            lk[w, pl.ds(at, LAGS), 256:512] = (v * cos - u * sin).astype(BF16)
        return carry

    def g_copy(w, k):
        return pltpu.make_async_remote_copy(
            gath.at[w, r], gath.at[w, r], g_send.at[w, k], g_recv.at[w, k],
            device_id={"chan": c, "rep": jnp.bitwise_xor(r, k)}, device_id_type=MESH,
        )

    def own_part(w):
        wait_all(recv.at[w, pl.ds(0, chans - 1)], a_send.at[w], a_recv.at[w])
        re, im = whiten(recv.at[w], dft, absbuf, xbuf, normed)
        mask = jnp.zeros((1, 128), F32)
        for q in range(reps):
            tile = chan_live[w][:, (q // 2) * 128 : (q // 2) * 128 + 128]
            mask = jnp.where(r == q, pltpu.roll(tile, (64 * q) % 128, 1), mask)
        re, im = re * mask, im * mask
        gath[w, r] = jnp.where(iota((K, 128), 1) < 64, re, pltpu.roll(im, 64, 1)).astype(BF16)
        for k in (2, 3, 1):
            g_copy(w, k).start()

    def correlate(w):
        for k in range(1, reps):
            g_copy(w, k).wait_recv()
            g_copy(w, k).wait_send()
        low = iota((K, 128), 1) < 64
        for h in range(2):
            a, b = gath[w, 2 * h], gath[w, 2 * h + 1]
            rhs[0:K, h * 128 : h * 128 + 128] = jnp.where(low, a, swap(b))
            rhs[K:, h * 128 : h * 128 + 128] = jnp.where(low, swap(a), b)

        part = jnp.dot(lk[w], rhs[...], preferred_element_type=F32)
        for k in range(out.shape[0]):
            piece = part[k * LAGS : (k + 1) * LAGS]
            if w == 0:
                out[k] = piece
            else:
                out[k] = (out[k] + piece) * inv[k : k + 1, :]

    own_part(0)
    wait_all(srcbuf.at[pl.ds(0, (nyx - 1) * Z)], y_send, y_recv)
    re, im = whiten(srcbuf, dft, absbuf, xbuf, normed)
    ls_col = jnp.concatenate([ls[0], ls[1]], axis=0)[:, :1]
    for part, value in enumerate((re, im)):
        rows = jnp.transpose(value)[:64] * ls_col
        srcspec[part] = rows.astype(BF16).astype(F32)

    lax.fori_loop(0, 32, lag_rows, 0)

    own_part(1)
    correlate(0)
    correlate(1)


def solution(mesh):
    chans, reps = mesh.shape["chan"], mesh.shape["rep"]

    def shards(records, sources, dead_list):
        windows, groups, width, span = records.shape
        length = span * chans
        dft, lag = tables(length)
        quarter = sources.shape[0] // reps
        vmem = pl.BlockSpec(memory_space=pltpu.VMEM)
        hbm = pl.BlockSpec(memory_space=pltpu.HBM)
        dma = pltpu.SemaphoreType.DMA
        return pl.pallas_call(
            functools.partial(gather_kernel, chans, reps),
            out_shape=jax.ShapeDtypeStruct((quarter, LAGS, 256), F32),
            in_specs=[hbm] * 5,
            out_specs=vmem,
            scratch_shapes=[
                pltpu.VMEM((windows, groups, span, width), BF16),
                pltpu.VMEM((1, sources.shape[0]), jnp.int32),
                pltpu.VMEM(dead_list.shape, jnp.int32),
                pltpu.VMEM((512, length), BF16),
                pltpu.VMEM((2, LAGS, K), F32),
                pltpu.VMEM((2, chans, 16, 128), BF16),
                pltpu.VMEM((2, chans, 16, 128), BF16),
                pltpu.VMEM((chans * 16, 256), F32),
                pltpu.VMEM((reps, 16, 128), BF16),
                pltpu.VMEM((reps, 16, 128), BF16),
                pltpu.VMEM((chans, 16, 128), BF16),
                pltpu.VMEM((2, reps, K, 128), BF16),
                pltpu.VMEM((2 * K, 256), BF16),
                pltpu.VMEM((2, quarter * LAGS, 2 * K), BF16),
                pltpu.VMEM((quarter, 256), F32),
                pltpu.VMEM((length // 2 + 128, 128), BF16),
                pltpu.VMEM((length // 2, 128), BF16),
                pltpu.VMEM((length // 2, 128), BF16),
                pltpu.VMEM((2, 64, 256), F32),
                pltpu.VMEM((2, 128, 128), F32),
                dma((6,)), dma((2,)), dma((2,)), dma((reps,)), dma((reps,)),
                dma, dma, dma, dma, dma((2, reps)), dma((2, reps)),
            ],
            compiler_params=pltpu.CompilerParams(
                collective_id=0, has_side_effects=True, vmem_limit_bytes=48 << 20
            ),
            name="correlations",
        )(
            *[
                pltpu.with_memory_space_constraint(x, pltpu.HBM)
                for x in (
                    jnp.transpose(records, (0, 1, 3, 2)),
                    sources.reshape(1, -1),
                    dead_list,
                    jnp.asarray(dft),
                    jnp.asarray(lag),
                )
            ]
        )

    return jax.shard_map(
        shards,
        mesh=mesh,
        in_specs=(P(None, None, "rep", "chan"), P(), P()),
        out_specs=P("rep", None, "chan"),
        check_vma=False,
    )
```

```python
import functools
import math

import jax
import jax.numpy as jnp
import numpy as np
from jax import lax
from jax.experimental import pallas as pl
from jax.experimental.pallas import tpu as pltpu
from jax.sharding import PartitionSpec as P

K = 256
K0 = 16
HALF = 32
WH = 32
LAGS = 64
EPS = 1e-06
Z = 8

MESH = pl.DeviceIdType.MESH
BF16 = jnp.bfloat16
F32 = jnp.float32


def tables(length):
    m = ((K0 + np.arange(K))[:, None] * np.arange(length)[None, :]) % length
    angle = m.astype(np.float64) * (2.0 * math.pi / length)
    dft = np.concatenate([np.cos(angle), -np.sin(angle)], axis=0).astype(jnp.bfloat16)
    tau = np.arange(LAGS)[:, None] - LAGS // 2
    phi = ((tau * (K0 + np.arange(K))[None, :]) % length).astype(np.float64) * (2.0 * math.pi / length)
    lag = np.stack([np.cos(phi), np.sin(phi)]).astype(np.float32)
    return dft, lag


def iota(shape, axis):
    return lax.broadcasted_iota(jnp.int32, shape, axis)


def swap(x):
    return pltpu.roll(x, 64, 1)


def whiten(buf, dft, absbuf, xbuf, normed):
    blocks = buf.shape[0]
    top = blocks * 16
    low = iota((16, 128), 1) < 64

    def spread(b, carry):
        for i in range(8):
            at = b * 8 + i
            first, second = buf[at], buf[at + blocks // 2]
            x0 = jnp.where(low, first, swap(second))
            x1 = jnp.where(low, swap(first), second)
            rows = pl.multiple_of(at * 32, 32)
            xbuf[pl.ds(rows, 16), :] = x0
            xbuf[pl.ds(rows + 16, 16), :] = x1
            absbuf[pl.ds(rows + 64, 16), :] = jnp.abs(x0)
            absbuf[pl.ds(rows + 80, 16), :] = jnp.abs(x1)
        return carry

    lax.fori_loop(0, blocks // 16, spread, 0)
    low = iota((64, 128), 1) < 64
    zero = jnp.zeros((64, 128), BF16)
    absbuf[0:64, :] = jnp.where(low, zero, swap(absbuf[top : top + 64, :]))
    absbuf[top + 64 :, :] = jnp.where(low, swap(absbuf[64:128, :]), zero)
    band = (jnp.abs(iota((128, 256), 1) - 64 - iota((128, 256), 0)) <= HALF).astype(BF16)

    for b in range(top // 128):
        start = b * 128
        total = jnp.dot(band, absbuf[pl.ds(start, 256), :], preferred_element_type=F32)
        t = iota((128, 128), 0) + b * 128 + jnp.where(iota((128, 128), 1) < 64, 0, top)
        n = (jnp.minimum(t, HALF) + jnp.minimum(2 * top - 1 - t, HALF) + 1).astype(F32)
        x = xbuf[pl.ds(start, 128), :].astype(F32)
        normed[pl.ds(start, 128), :] = (x * n / (total + EPS * n)).astype(BF16)
    x = normed[...]
    spectrum = jnp.dot(dft[:, :top], x, preferred_element_type=F32)
    other = jnp.dot(dft[:, top:], x, preferred_element_type=F32)
    spectrum = spectrum + pltpu.roll(other, 64, 1)
    re, im = spectrum[:K], spectrum[K:]
    amp = jnp.sqrt(re * re + im * im)
    high = amp.astype(BF16)
    rest = amp - high.astype(F32)
    mid = rest.astype(BF16)
    near = (jnp.abs(iota((K, K), 0) - iota((K, K), 1)) <= WH).astype(BF16)
    total = jnp.dot(near, mid, preferred_element_type=F32) + jnp.dot(near, high, preferred_element_type=F32)
    j = iota((K, 128), 0)
    n = (jnp.minimum(j, WH) + jnp.minimum(K - 1 - j, WH) + 1).astype(F32)
    scale = 1.0 / (total / n + EPS)
    return re * scale, im * scale


def gather_kernel(
    chans, reps,
    rec_hbm, src_hbm, dead_hbm, dft_hbm, lag_hbm,
    out, lk1, rhs, inv,
    rec, src_ref, dead_ref, dft, lag,
    packed, recv, cols, picks, pickrecv, srcbuf, gath, rhs0, lk0, absbuf, xbuf, normed, srcspec, livesrc,
    sem_in, a_send, a_recv, p_send, p_recv, z_send, z_recv, y_send, y_recv, g_send, g_recv,
):
    c, r = lax.axis_index("chan"), lax.axis_index("rep")
    z, yx = lax.rem(c, Z), c // Z
    nyx = chans // Z
    barrier = pltpu.get_barrier_semaphore()

    loads = [
        pltpu.make_async_copy(a, b, sem_in.at[i])
        for i, (a, b) in enumerate(
            [
                (rec_hbm.at[0], rec.at[0]), (src_hbm, src_ref), (dead_hbm, dead_ref), (dft_hbm, dft), (lag_hbm, lag),
                (rec_hbm.at[1], rec.at[1]),
            ]
        )
    ]
    for i in (0, 5, 1, 2, 3, 4):
        loads[i].start()

    def greet(k, carry):
        pl.semaphore_signal(barrier, inc=1, device_id={"chan": lax.rem(c + k, chans), "rep": r}, device_id_type=MESH)
        return carry

    lax.fori_loop(1, chans, greet, 0)
    for k in range(1, reps):
        pl.semaphore_signal(barrier, inc=1, device_id={"chan": c, "rep": lax.rem(r + k, reps)}, device_id_type=MESH)

    loads[0].wait()

    def pack_window(w):
        def pack(i, carry):
            for k in range(8):
                g = i * 8 + k
                packed[w, g] = jnp.concatenate([rec[w, g, 0:16], rec[w, g, 16:32]], axis=1)
            return carry

        lax.fori_loop(0, chans // 8, pack, 0)
        recv[w, c] = packed[w, c]

    pack_window(0)
    pl.semaphore_wait(barrier, chans - 1 + reps - 1)

    some_zero, some_one = chans * 3 // 8, chans * 5 // 8

    def send_part(w, first, last):
        def send(k, carry):
            d = lax.rem(c + k, chans)
            pltpu.make_async_remote_copy(
                packed.at[w, d], recv.at[w, c], a_send.at[w], a_recv.at[w],
                device_id={"chan": d, "rep": r}, device_id_type=MESH,
            ).start()
            return carry

        lax.fori_loop(first, last, send, 0)

    send_part(0, 1, some_zero)
    loads[5].wait()
    pack_window(1)

    loads[1].wait()
    src = src_ref[...]
    within = src & 255
    mine = jnp.where((within >> 6) == r, within & 63, -1000)
    row = iota((128, 128), 0)
    sel = jnp.concatenate([(row == mine).astype(BF16), (row - 64 == mine).astype(BF16)], axis=1)
    block = src >> 8
    block2 = jnp.concatenate([block, block], axis=1)
    accs = []
    for w in range(2):
        cols[...] = jnp.dot(packed[w].reshape(chans * 16, 128), sel, preferred_element_type=F32)

        def pick(i, acc):
            for k in range(8):
                g = i * 8 + k
                part = cols[pl.ds(pl.multiple_of(g * 16, 16), 16), :]
                acc = acc + jnp.where(block2 == g, part, 0.0)
            return acc

        accs.append(lax.fori_loop(0, chans // 8, pick, jnp.zeros((16, 256), F32)))
    lane = iota((16, 128), 1)
    for q in range(reps):
        value = jnp.zeros((16, 128), F32)
        for th in range(2):
            for w in range(2):
                to = th * 64 + w * 32
                piece = pltpu.roll(accs[w][:, th * 128 : th * 128 + 128], (to - 32 * q) % 128, 1)
                value = jnp.where((lane >= to) & (lane < to + 32), piece, value)
        picks[q] = value.astype(BF16)
    pickrecv[r] = picks[r]

    def p_copy(k):
        d = lax.rem(r + k, reps)
        return pltpu.make_async_remote_copy(
            picks.at[d], pickrecv.at[r], p_send.at[k], p_recv.at[k], device_id={"chan": c, "rep": d}, device_id_type=MESH
        )

    for k in range(1, reps):
        p_copy(k).start()
    send_part(0, some_zero, chans)

    loads[2].wait()
    dead = dead_ref[...]
    eye = iota((128, 128), 0) == iota((128, 128), 1)
    src_col = jnp.sum(jnp.where(eye, jnp.broadcast_to(src, (128, 128)), 0), axis=1, keepdims=True)
    ones = jnp.ones((8, 1024), BF16)
    chan_live = []
    for w in range(2):
        listed = dead[w : w + 1, :]
        hit = jnp.sum((listed == src_col).astype(F32), axis=1, keepdims=True)
        livesrc[w] = jnp.broadcast_to(jnp.where(hit > 0.5, 0.0, 1.0), (128, 128))
        here = jnp.where((listed >> 8) == c, listed & 255, -1)
        onehot = (iota((256, 1024), 0) == here).astype(BF16)
        hits = lax.dot_general(ones, onehot, (((1,), (1,)), ((), ())), preferred_element_type=F32)
        chan_live.append(jnp.where(hits[0:1] > 0.5, 0.0, 1.0))
    start = pl.multiple_of(r * 32, 32)
    ls = [livesrc[w, pl.ds(start, 32), :] for w in range(2)]
    for h in range(2):
        span = slice(h * 128, h * 128 + 128)
        pairs = ls[0] * chan_live[0][:, span] + ls[1] * chan_live[1][:, span]
        inv[:, span] = 1.0 / (math.sqrt(K) * jnp.maximum(pairs, 1.0))

    for k in range(1, reps):
        p_copy(k).wait_send()
        p_copy(k).wait_recv()
    total = pickrecv[0].astype(F32)
    for q in range(1, reps):
        total = total + pickrecv[q].astype(F32)
    srcbuf[c] = total.astype(BF16)

    def z_start(k, carry):
        pltpu.make_async_remote_copy(
            srcbuf.at[c], srcbuf.at[c], z_send, z_recv,
            device_id={"chan": yx * Z + lax.rem(z + k, Z), "rep": r}, device_id_type=MESH,
        ).start()
        return carry

    def y_start(k, carry):
        span = srcbuf.at[pl.ds(yx * Z, Z)]
        pltpu.make_async_remote_copy(
            span, span, y_send, y_recv,
            device_id={"chan": lax.rem(yx + k, nyx) * Z + z, "rep": r}, device_id_type=MESH,
        ).start()
        return carry

    def wait_all(some, send, recv):
        bulk = pltpu.make_async_remote_copy(
            some, some, send, recv, device_id={"chan": c, "rep": lax.rem(r + 1, reps)}, device_id_type=MESH
        )
        bulk.wait_send()
        bulk.wait_recv()

    lax.fori_loop(1, Z, z_start, 0)
    send_part(1, 1, some_one)
    wait_all(srcbuf.at[pl.ds(0, Z - 1)], z_send, z_recv)
    lax.fori_loop(1, nyx, y_start, 0)
    send_part(1, some_one, chans)
    loads[3].wait()
    loads[4].wait()
    def lag_rows(s, carry):
        at = pl.multiple_of(s * LAGS, LAGS)
        for w in range(2):
            u = srcspec[0, pl.ds(w * 32 + s, 1), :]
            v = srcspec[1, pl.ds(w * 32 + s, 1), :]
            cos, sin = lag[0], lag[1]
            lk = lk1 if w else lk0
            lk[pl.ds(at, LAGS), 0:256] = (u * cos + v * sin).astype(BF16)
            lk[pl.ds(at, LAGS), 256:512] = (v * cos - u * sin).astype(BF16)
        return carry

    def g_copy(w, k):
        return pltpu.make_async_remote_copy(
            gath.at[w, r], gath.at[w, r], g_send.at[w, k], g_recv.at[w, k],
            device_id={"chan": c, "rep": jnp.bitwise_xor(r, k)}, device_id_type=MESH,
        )

    def own_part(w):
        wait_all(recv.at[w, pl.ds(0, chans - 1)], a_send.at[w], a_recv.at[w])
        re, im = whiten(recv.at[w], dft, absbuf, xbuf, normed)
        mask = jnp.zeros((1, 128), F32)
        for q in range(reps):
            tile = chan_live[w][:, (q // 2) * 128 : (q // 2) * 128 + 128]
            mask = jnp.where(r == q, pltpu.roll(tile, (64 * q) % 128, 1), mask)
        re, im = re * mask, im * mask
        gath[w, r] = jnp.where(iota((K, 128), 1) < 64, re, pltpu.roll(im, 64, 1)).astype(BF16)
        for k in (2, 3, 1):
            g_copy(w, k).start()

    def correlate(w):
        for k in range(1, reps):
            g_copy(w, k).wait_recv()
            g_copy(w, k).wait_send()
        low = iota((K, 128), 1) < 64
        to = rhs if w else rhs0
        for h in range(2):
            a, b = gath[w, 2 * h], gath[w, 2 * h + 1]
            to[0:K, h * 128 : h * 128 + 128] = jnp.where(low, a, swap(b))
            to[K:, h * 128 : h * 128 + 128] = jnp.where(low, swap(a), b)
        if w == 0:
            part = jnp.dot(lk0[...], rhs0[...], preferred_element_type=F32)
            for k in range(out.shape[0]):
                out[k] = part[k * LAGS : (k + 1) * LAGS]

    own_part(0)
    wait_all(srcbuf.at[pl.ds(0, (nyx - 1) * Z)], y_send, y_recv)
    re, im = whiten(srcbuf, dft, absbuf, xbuf, normed)
    ls_col = jnp.concatenate([ls[0], ls[1]], axis=0)[:, :1]
    for part, value in enumerate((re, im)):
        rows = jnp.transpose(value)[:64] * ls_col
        srcspec[part] = rows.astype(BF16).astype(F32)

    lax.fori_loop(0, 32, lag_rows, 0)

    own_part(1)
    correlate(0)
    correlate(1)


def correlate_kernel(part, lk, rhs, inv, out):
    count = out.shape[0]
    first = pl.program_id(0) * count
    rows = pl.ds(pl.multiple_of(first * LAGS, count * LAGS), count * LAGS)
    summed = jnp.dot(lk[rows, :], rhs[...], preferred_element_type=F32)
    for k in range(count):
        out[k] = (part[first + k] + summed[k * LAGS : (k + 1) * LAGS]) * inv[pl.ds(first + k, 1), :]


def solution(mesh):
    chans, reps = mesh.shape["chan"], mesh.shape["rep"]

    def shards(records, sources, dead_list):
        windows, groups, width, span = records.shape
        length = span * chans
        dft, lag = tables(length)
        quarter = sources.shape[0] // reps
        vmem = pl.BlockSpec(memory_space=pltpu.VMEM)
        hbm = pl.BlockSpec(memory_space=pltpu.HBM)
        dma = pltpu.SemaphoreType.DMA
        partial = pl.pallas_call(
            functools.partial(gather_kernel, chans, reps),
            out_shape=[
                jax.ShapeDtypeStruct((quarter, LAGS, 256), F32),
                jax.ShapeDtypeStruct((quarter * LAGS, 2 * K), BF16),
                jax.ShapeDtypeStruct((2 * K, 256), BF16),
                jax.ShapeDtypeStruct((quarter, 256), F32),
            ],
            in_specs=[hbm] * 5,
            out_specs=[vmem] * 4,
            scratch_shapes=[
                pltpu.VMEM((windows, groups, span, width), BF16),
                pltpu.VMEM((1, sources.shape[0]), jnp.int32),
                pltpu.VMEM(dead_list.shape, jnp.int32),
                pltpu.VMEM((512, length), BF16),
                pltpu.VMEM((2, LAGS, K), F32),
                pltpu.VMEM((2, chans, 16, 128), BF16),
                pltpu.VMEM((2, chans, 16, 128), BF16),
                pltpu.VMEM((chans * 16, 256), F32),
                pltpu.VMEM((reps, 16, 128), BF16),
                pltpu.VMEM((reps, 16, 128), BF16),
                pltpu.VMEM((chans, 16, 128), BF16),
                pltpu.VMEM((2, reps, K, 128), BF16),
                pltpu.VMEM((2 * K, 256), BF16),
                pltpu.VMEM((quarter * LAGS, 2 * K), BF16),
                pltpu.VMEM((length // 2 + 128, 128), BF16),
                pltpu.VMEM((length // 2, 128), BF16),
                pltpu.VMEM((length // 2, 128), BF16),
                pltpu.VMEM((2, 64, 256), F32),
                pltpu.VMEM((2, 128, 128), F32),
                dma((6,)), dma((2,)), dma((2,)), dma((reps,)), dma((reps,)),
                dma, dma, dma, dma, dma((2, reps)), dma((2, reps)),
            ],
            compiler_params=pltpu.CompilerParams(
                collective_id=0, has_side_effects=True, vmem_limit_bytes=48 << 20
            ),
            name="correlations",
        )(
            *[
                pltpu.with_memory_space_constraint(x, pltpu.HBM)
                for x in (
                    jnp.transpose(records, (0, 1, 3, 2)),
                    sources.reshape(1, -1),
                    dead_list,
                    jnp.asarray(dft),
                    jnp.asarray(lag),
                )
            ]
        )
        step = 16
        return pl.pallas_call(
            correlate_kernel,
            grid=(quarter // step,),
            out_shape=jax.ShapeDtypeStruct((quarter, LAGS, 256), F32),
            in_specs=[vmem] * 4,
            out_specs=pl.BlockSpec((step, LAGS, 256), lambda i: (i, 0, 0)),
            compiler_params=pltpu.CompilerParams(vmem_limit_bytes=16 << 20),
            name="correlate",
        )(*partial)

    return jax.shard_map(
        shards,
        mesh=mesh,
        in_specs=(P(None, None, "rep", "chan"), P(), P()),
        out_specs=P("rep", None, "chan"),
        check_vma=False,
    )
```

```python
import functools
import math

import jax
import jax.numpy as jnp
import numpy as np
from jax import lax
from jax.experimental import pallas as pl
from jax.experimental.pallas import tpu as pltpu
from jax.sharding import PartitionSpec as P

K = 256
K0 = 16
HALF = 32
WH = 32
LAGS = 64
EPS = 1e-06
Z = 8

MESH = pl.DeviceIdType.MESH
BF16 = jnp.bfloat16
F32 = jnp.float32


def tables(length):
    m = ((K0 + np.arange(K))[:, None] * np.arange(length)[None, :]) % length
    angle = m.astype(np.float64) * (2.0 * math.pi / length)
    dft = np.concatenate([np.cos(angle), -np.sin(angle)], axis=0).astype(jnp.bfloat16)
    tau = np.arange(LAGS)[:, None] - LAGS // 2
    phi = ((tau * (K0 + np.arange(K))[None, :]) % length).astype(np.float64) * (2.0 * math.pi / length)
    lag = np.stack([np.cos(phi), np.sin(phi)]).astype(np.float32)
    return dft, lag


def iota(shape, axis):
    return lax.broadcasted_iota(jnp.int32, shape, axis)


def swap(x):
    return pltpu.roll(x, 64, 1)


def whiten(buf, dft, absbuf, xbuf, normed):
    blocks = buf.shape[0]
    top = blocks * 16
    low = iota((16, 128), 1) < 64

    def spread(b, carry):
        for i in range(8):
            at = b * 8 + i
            first, second = buf[at], buf[at + blocks // 2]
            x0 = jnp.where(low, first, swap(second))
            x1 = jnp.where(low, swap(first), second)
            rows = pl.multiple_of(at * 32, 32)
            xbuf[pl.ds(rows, 16), :] = x0
            xbuf[pl.ds(rows + 16, 16), :] = x1
            absbuf[pl.ds(rows + 64, 16), :] = jnp.abs(x0)
            absbuf[pl.ds(rows + 80, 16), :] = jnp.abs(x1)
        return carry

    lax.fori_loop(0, blocks // 16, spread, 0)
    low = iota((64, 128), 1) < 64
    zero = jnp.zeros((64, 128), BF16)
    absbuf[0:64, :] = jnp.where(low, zero, swap(absbuf[top : top + 64, :]))
    absbuf[top + 64 :, :] = jnp.where(low, swap(absbuf[64:128, :]), zero)
    band = (jnp.abs(iota((128, 256), 1) - 64 - iota((128, 256), 0)) <= HALF).astype(BF16)

    for b in range(top // 128):
        start = b * 128
        total = jnp.dot(band, absbuf[pl.ds(start, 256), :], preferred_element_type=F32)
        t = iota((128, 128), 0) + b * 128 + jnp.where(iota((128, 128), 1) < 64, 0, top)
        n = (jnp.minimum(t, HALF) + jnp.minimum(2 * top - 1 - t, HALF) + 1).astype(F32)
        x = xbuf[pl.ds(start, 128), :].astype(F32)
        normed[pl.ds(start, 128), :] = (x * n / (total + EPS * n)).astype(BF16)
    x = normed[...]
    spectrum = jnp.dot(dft[:, :top], x, preferred_element_type=F32)
    other = jnp.dot(dft[:, top:], x, preferred_element_type=F32)
    spectrum = spectrum + pltpu.roll(other, 64, 1)
    re, im = spectrum[:K], spectrum[K:]
    amp = jnp.sqrt(re * re + im * im)
    high = amp.astype(BF16)
    rest = amp - high.astype(F32)
    mid = rest.astype(BF16)
    near = (jnp.abs(iota((K, K), 0) - iota((K, K), 1)) <= WH).astype(BF16)
    total = jnp.dot(near, mid, preferred_element_type=F32) + jnp.dot(near, high, preferred_element_type=F32)
    j = iota((K, 128), 0)
    n = (jnp.minimum(j, WH) + jnp.minimum(K - 1 - j, WH) + 1).astype(F32)
    scale = 1.0 / (total / n + EPS)
    return re * scale, im * scale


def gather_kernel(
    chans, reps,
    rec_hbm, src_hbm, dead_hbm, dft_hbm, lag_hbm,
    out, lk1, rhs, inv,
    rec, src_ref, dead_ref, dft, lag,
    packed, recv, cols, picks, pickrecv, srcbuf, gath, rhs0, lk0, absbuf, xbuf, normed, srcspec, livesrc,
    sem_in, a_send, a_recv, p_send, p_recv, z_send, z_recv, y_send, y_recv, g_send, g_recv,
):
    c, r = lax.axis_index("chan"), lax.axis_index("rep")
    z, yx = lax.rem(c, Z), c // Z
    nyx = chans // Z
    barrier = pltpu.get_barrier_semaphore()

    loads = [
        pltpu.make_async_copy(a, b, sem_in.at[i])
        for i, (a, b) in enumerate(
            [
                (rec_hbm.at[0], rec.at[0]), (src_hbm, src_ref), (dead_hbm, dead_ref), (dft_hbm, dft), (lag_hbm, lag),
                (rec_hbm.at[1], rec.at[1]),
            ]
        )
    ]
    for i in (0, 5, 1, 2, 3, 4):
        loads[i].start()

    def greet(k, carry):
        pl.semaphore_signal(barrier, inc=1, device_id={"chan": lax.rem(c + k, chans), "rep": r}, device_id_type=MESH)
        return carry

    lax.fori_loop(1, chans, greet, 0)
    for k in range(1, reps):
        pl.semaphore_signal(barrier, inc=1, device_id={"chan": c, "rep": lax.rem(r + k, reps)}, device_id_type=MESH)

    loads[0].wait()

    def pack_window(w):
        def pack(i, carry):
            for k in range(8):
                g = i * 8 + k
                packed[w, g] = jnp.concatenate([rec[w, g, 0:16], rec[w, g, 16:32]], axis=1)
            return carry

        lax.fori_loop(0, chans // 8, pack, 0)
        recv[w, c] = packed[w, c]

    pack_window(0)
    pl.semaphore_wait(barrier, chans - 1 + reps - 1)

    some_zero, some_one = chans * 3 // 8, chans * 5 // 8

    def send_part(w, first, last):
        def send(k, carry):
            d = lax.rem(c + k, chans)
            pltpu.make_async_remote_copy(
                packed.at[w, d], recv.at[w, c], a_send.at[w], a_recv.at[w],
                device_id={"chan": d, "rep": r}, device_id_type=MESH,
            ).start()
            return carry

        lax.fori_loop(first, last, send, 0)

    send_part(0, 1, some_zero)
    loads[5].wait()
    pack_window(1)

    loads[1].wait()
    src = src_ref[...]
    within = src & 255
    mine = jnp.where((within >> 6) == r, within & 63, -1000)
    row = iota((128, 128), 0)
    sel = jnp.concatenate([(row == mine).astype(BF16), (row - 64 == mine).astype(BF16)], axis=1)
    block = src >> 8
    block2 = jnp.concatenate([block, block], axis=1)
    accs = []
    for w in range(2):
        cols[...] = jnp.dot(packed[w].reshape(chans * 16, 128), sel, preferred_element_type=F32)

        def pick(i, acc):
            for k in range(8):
                g = i * 8 + k
                part = cols[pl.ds(pl.multiple_of(g * 16, 16), 16), :]
                acc = acc + jnp.where(block2 == g, part, 0.0)
            return acc

        accs.append(lax.fori_loop(0, chans // 8, pick, jnp.zeros((16, 256), F32)))
    lane = iota((16, 128), 1)
    for q in range(reps):
        value = jnp.zeros((16, 128), F32)
        for th in range(2):
            for w in range(2):
                to = th * 64 + w * 32
                piece = pltpu.roll(accs[w][:, th * 128 : th * 128 + 128], (to - 32 * q) % 128, 1)
                value = jnp.where((lane >= to) & (lane < to + 32), piece, value)
        picks[q] = value.astype(BF16)
    pickrecv[r] = picks[r]

    def p_copy(k):
        d = lax.rem(r + k, reps)
        return pltpu.make_async_remote_copy(
            picks.at[d], pickrecv.at[r], p_send.at[k], p_recv.at[k], device_id={"chan": c, "rep": d}, device_id_type=MESH
        )

    for k in range(1, reps):
        p_copy(k).start()
    send_part(0, some_zero, chans)

    loads[2].wait()
    dead = dead_ref[...]
    eye = iota((128, 128), 0) == iota((128, 128), 1)
    src_col = jnp.sum(jnp.where(eye, jnp.broadcast_to(src, (128, 128)), 0), axis=1, keepdims=True)
    ones = jnp.ones((8, 1024), BF16)
    chan_live = []
    for w in range(2):
        listed = dead[w : w + 1, :]
        hit = jnp.sum((listed == src_col).astype(F32), axis=1, keepdims=True)
        livesrc[w] = jnp.broadcast_to(jnp.where(hit > 0.5, 0.0, 1.0), (128, 128))
        here = jnp.where((listed >> 8) == c, listed & 255, -1)
        onehot = (iota((256, 1024), 0) == here).astype(BF16)
        hits = lax.dot_general(ones, onehot, (((1,), (1,)), ((), ())), preferred_element_type=F32)
        chan_live.append(jnp.where(hits[0:1] > 0.5, 0.0, 1.0))
    start = pl.multiple_of(r * 32, 32)
    ls = [livesrc[w, pl.ds(start, 32), :] for w in range(2)]
    for h in range(2):
        span = slice(h * 128, h * 128 + 128)
        pairs = ls[0] * chan_live[0][:, span] + ls[1] * chan_live[1][:, span]
        inv[:, span] = 1.0 / (math.sqrt(K) * jnp.maximum(pairs, 1.0))

    for k in range(1, reps):
        p_copy(k).wait_send()
        p_copy(k).wait_recv()
    total = pickrecv[0].astype(F32)
    for q in range(1, reps):
        total = total + pickrecv[q].astype(F32)
    srcbuf[c] = total.astype(BF16)

    def z_start(k, carry):
        pltpu.make_async_remote_copy(
            srcbuf.at[c], srcbuf.at[c], z_send, z_recv,
            device_id={"chan": yx * Z + lax.rem(z + k, Z), "rep": r}, device_id_type=MESH,
        ).start()
        return carry

    def y_start(k, carry):
        span = srcbuf.at[pl.ds(yx * Z, Z)]
        pltpu.make_async_remote_copy(
            span, span, y_send, y_recv,
            device_id={"chan": lax.rem(yx + k, nyx) * Z + z, "rep": r}, device_id_type=MESH,
        ).start()
        return carry

    sent = []

    def wait_all(some, send, recv):
        bulk = pltpu.make_async_remote_copy(
            some, some, send, recv, device_id={"chan": c, "rep": lax.rem(r + 1, reps)}, device_id_type=MESH
        )
        sent.append(bulk)
        bulk.wait_recv()

    lax.fori_loop(1, Z, z_start, 0)
    send_part(1, 1, some_one)
    wait_all(srcbuf.at[pl.ds(0, Z - 1)], z_send, z_recv)
    lax.fori_loop(1, nyx, y_start, 0)
    send_part(1, some_one, chans)
    loads[3].wait()
    loads[4].wait()
    def lag_rows(s, carry):
        at = pl.multiple_of(s * LAGS, LAGS)
        for w in range(2):
            u = srcspec[0, pl.ds(w * 32 + s, 1), :]
            v = srcspec[1, pl.ds(w * 32 + s, 1), :]
            cos, sin = lag[0], lag[1]
            lk = lk1 if w else lk0
            lk[pl.ds(at, LAGS), 0:256] = (u * cos + v * sin).astype(BF16)
            lk[pl.ds(at, LAGS), 256:512] = (v * cos - u * sin).astype(BF16)
        return carry

    def g_copy(w, k):
        return pltpu.make_async_remote_copy(
            gath.at[w, r], gath.at[w, r], g_send.at[w, k], g_recv.at[w, k],
            device_id={"chan": c, "rep": jnp.bitwise_xor(r, k)}, device_id_type=MESH,
        )

    def own_part(w):
        wait_all(recv.at[w, pl.ds(0, chans - 1)], a_send.at[w], a_recv.at[w])
        re, im = whiten(recv.at[w], dft, absbuf, xbuf, normed)
        mask = jnp.zeros((1, 128), F32)
        for q in range(reps):
            tile = chan_live[w][:, (q // 2) * 128 : (q // 2) * 128 + 128]
            mask = jnp.where(r == q, pltpu.roll(tile, (64 * q) % 128, 1), mask)
        re, im = re * mask, im * mask
        gath[w, r] = jnp.where(iota((K, 128), 1) < 64, re, pltpu.roll(im, 64, 1)).astype(BF16)
        for k in (2, 3, 1):
            g_copy(w, k).start()

    def correlate(w):
        for k in range(1, reps):
            g_copy(w, k).wait_recv()
            sent.append(g_copy(w, k))
        low = iota((K, 128), 1) < 64
        to = rhs if w else rhs0
        for h in range(2):
            a, b = gath[w, 2 * h], gath[w, 2 * h + 1]
            to[0:K, h * 128 : h * 128 + 128] = jnp.where(low, a, swap(b))
            to[K:, h * 128 : h * 128 + 128] = jnp.where(low, swap(a), b)
        if w == 0:
            part = jnp.dot(lk0[...], rhs0[...], preferred_element_type=F32)
            for k in range(out.shape[0]):
                out[k] = part[k * LAGS : (k + 1) * LAGS]

    own_part(0)
    own_part(1)
    wait_all(srcbuf.at[pl.ds(0, (nyx - 1) * Z)], y_send, y_recv)
    re, im = whiten(srcbuf, dft, absbuf, xbuf, normed)
    ls_col = jnp.concatenate([ls[0], ls[1]], axis=0)[:, :1]
    for part, value in enumerate((re, im)):
        rows = jnp.transpose(value)[:64] * ls_col
        srcspec[part] = rows.astype(BF16).astype(F32)

    lax.fori_loop(0, 32, lag_rows, 0)

    correlate(0)
    correlate(1)
    for bulk in sent:
        bulk.wait_send()


def correlate_kernel(part, lk, rhs, inv, out, buf, sem):
    parts = sem.shape[0]
    count = out.shape[0] // parts
    copies = []
    for p in range(parts):
        first = p * count
        summed = jnp.dot(lk[first * LAGS : (first + count) * LAGS, :], rhs[...], preferred_element_type=F32)
        for k in range(count):
            buf[first + k] = (part[first + k] + summed[k * LAGS : (k + 1) * LAGS]) * inv[first + k : first + k + 1, :]
        copies.append(pltpu.make_async_copy(buf.at[pl.ds(first, count)], out.at[pl.ds(first, count)], sem.at[p]))
        copies[-1].start()
    for copy in copies:
        copy.wait()


def solution(mesh):
    chans, reps = mesh.shape["chan"], mesh.shape["rep"]

    def shards(records, sources, dead_list):
        windows, groups, width, span = records.shape
        length = span * chans
        dft, lag = tables(length)
        quarter = sources.shape[0] // reps
        vmem = pl.BlockSpec(memory_space=pltpu.VMEM)
        hbm = pl.BlockSpec(memory_space=pltpu.HBM)
        dma = pltpu.SemaphoreType.DMA
        partial = pl.pallas_call(
            functools.partial(gather_kernel, chans, reps),
            out_shape=[
                jax.ShapeDtypeStruct((quarter, LAGS, 256), F32),
                jax.ShapeDtypeStruct((quarter * LAGS, 2 * K), BF16),
                jax.ShapeDtypeStruct((2 * K, 256), BF16),
                jax.ShapeDtypeStruct((quarter, 256), F32),
            ],
            in_specs=[hbm] * 5,
            out_specs=[vmem] * 4,
            scratch_shapes=[
                pltpu.VMEM((windows, groups, span, width), BF16),
                pltpu.VMEM((1, sources.shape[0]), jnp.int32),
                pltpu.VMEM(dead_list.shape, jnp.int32),
                pltpu.VMEM((512, length), BF16),
                pltpu.VMEM((2, LAGS, K), F32),
                pltpu.VMEM((2, chans, 16, 128), BF16),
                pltpu.VMEM((2, chans, 16, 128), BF16),
                pltpu.VMEM((chans * 16, 256), F32),
                pltpu.VMEM((reps, 16, 128), BF16),
                pltpu.VMEM((reps, 16, 128), BF16),
                pltpu.VMEM((chans, 16, 128), BF16),
                pltpu.VMEM((2, reps, K, 128), BF16),
                pltpu.VMEM((2 * K, 256), BF16),
                pltpu.VMEM((quarter * LAGS, 2 * K), BF16),
                pltpu.VMEM((length // 2 + 128, 128), BF16),
                pltpu.VMEM((length // 2, 128), BF16),
                pltpu.VMEM((length // 2, 128), BF16),
                pltpu.VMEM((2, 64, 256), F32),
                pltpu.VMEM((2, 128, 128), F32),
                dma((6,)), dma((2,)), dma((2,)), dma((reps,)), dma((reps,)),
                dma, dma, dma, dma, dma((2, reps)), dma((2, reps)),
            ],
            compiler_params=pltpu.CompilerParams(
                collective_id=0, has_side_effects=True, vmem_limit_bytes=48 << 20
            ),
            name="correlations",
        )(
            *[
                pltpu.with_memory_space_constraint(x, pltpu.HBM)
                for x in (
                    jnp.transpose(records, (0, 1, 3, 2)),
                    sources.reshape(1, -1),
                    dead_list,
                    jnp.asarray(dft),
                    jnp.asarray(lag),
                )
            ]
        )
        return pl.pallas_call(
            correlate_kernel,
            out_shape=jax.ShapeDtypeStruct((quarter, LAGS, 256), F32),
            in_specs=[vmem] * 4,
            out_specs=hbm,
            scratch_shapes=[pltpu.VMEM((quarter, LAGS, 256), F32), dma((4,))],
            compiler_params=pltpu.CompilerParams(vmem_limit_bytes=16 << 20),
            name="correlate",
        )(*partial)

    return jax.shard_map(
        shards,
        mesh=mesh,
        in_specs=(P(None, None, "rep", "chan"), P(), P()),
        out_specs=P("rep", None, "chan"),
        check_vma=False,
    )
```

```python
import functools
import math

import jax
import jax.numpy as jnp
import numpy as np
from jax import lax
from jax.experimental import pallas as pl
from jax.experimental.pallas import tpu as pltpu
from jax.sharding import PartitionSpec as P

K = 256
K0 = 16
HALF = 32
WH = 32
LAGS = 64
EPS = 1e-06
Z = 8

MESH = pl.DeviceIdType.MESH
BF16 = jnp.bfloat16
F32 = jnp.float32


def tables(length):
    m = ((K0 + np.arange(K))[:, None] * np.arange(length)[None, :]) % length
    angle = m.astype(np.float64) * (2.0 * math.pi / length)
    dft = np.concatenate([np.cos(angle), -np.sin(angle)], axis=0).astype(jnp.bfloat16)
    tau = np.arange(LAGS)[:, None] - LAGS // 2
    phi = ((tau * (K0 + np.arange(K))[None, :]) % length).astype(np.float64) * (2.0 * math.pi / length)
    lag = np.stack([np.cos(phi), np.sin(phi)]).astype(np.float32)
    return dft, lag


def iota(shape, axis):
    return lax.broadcasted_iota(jnp.int32, shape, axis)


def swap(x):
    return pltpu.roll(x, 64, 1)


def whiten(buf, dft, absbuf, xbuf, normed):
    blocks = buf.shape[0]
    top = blocks * 16
    low = iota((16, 128), 1) < 64

    def spread(b, carry):
        for i in range(8):
            at = b * 8 + i
            first, second = buf[at], buf[at + blocks // 2]
            x0 = jnp.where(low, first, swap(second))
            x1 = jnp.where(low, swap(first), second)
            rows = pl.multiple_of(at * 32, 32)
            xbuf[pl.ds(rows, 16), :] = x0
            xbuf[pl.ds(rows + 16, 16), :] = x1
            absbuf[pl.ds(rows + 64, 16), :] = jnp.abs(x0)
            absbuf[pl.ds(rows + 80, 16), :] = jnp.abs(x1)
        return carry

    lax.fori_loop(0, blocks // 16, spread, 0)
    low = iota((64, 128), 1) < 64
    zero = jnp.zeros((64, 128), BF16)
    absbuf[0:64, :] = jnp.where(low, zero, swap(absbuf[top : top + 64, :]))
    absbuf[top + 64 :, :] = jnp.where(low, swap(absbuf[64:128, :]), zero)
    band = (jnp.abs(iota((128, 256), 1) - 64 - iota((128, 256), 0)) <= HALF).astype(BF16)

    for b in range(top // 128):
        start = b * 128
        total = jnp.dot(band, absbuf[pl.ds(start, 256), :], preferred_element_type=F32)
        t = iota((128, 128), 0) + b * 128 + jnp.where(iota((128, 128), 1) < 64, 0, top)
        n = (jnp.minimum(t, HALF) + jnp.minimum(2 * top - 1 - t, HALF) + 1).astype(F32)
        x = xbuf[pl.ds(start, 128), :].astype(F32)
        normed[pl.ds(start, 128), :] = (x * n / (total + EPS * n)).astype(BF16)
    x = normed[...]
    spectrum = jnp.dot(dft[:, :top], x, preferred_element_type=F32)
    other = jnp.dot(dft[:, top:], x, preferred_element_type=F32)
    spectrum = spectrum + pltpu.roll(other, 64, 1)
    re, im = spectrum[:K], spectrum[K:]
    amp = jnp.sqrt(re * re + im * im)
    high = amp.astype(BF16)
    rest = amp - high.astype(F32)
    mid = rest.astype(BF16)
    near = (jnp.abs(iota((K, K), 0) - iota((K, K), 1)) <= WH).astype(BF16)
    total = jnp.dot(near, mid, preferred_element_type=F32) + jnp.dot(near, high, preferred_element_type=F32)
    j = iota((K, 128), 0)
    n = (jnp.minimum(j, WH) + jnp.minimum(K - 1 - j, WH) + 1).astype(F32)
    scale = 1.0 / (total / n + EPS)
    return re * scale, im * scale


def gather_kernel(
    chans, reps,
    rec_hbm, src_hbm, dead_hbm, dft_hbm, lag_hbm,
    out, lk1, rhs, inv,
    rec, src_ref, dead_ref, dft, lag,
    packed, recv, cols, picks, pickrecv, srcbuf, gath, rhs0, lk0, absbuf, xbuf, normed, srcspec, livesrc,
    sem_in, a_send, a_recv, p_send, p_recv, z_send, z_recv, y_send, y_recv, g_send, g_recv,
):
    c, r = lax.axis_index("chan"), lax.axis_index("rep")
    z, yx = lax.rem(c, Z), c // Z
    nyx = chans // Z
    barrier = pltpu.get_barrier_semaphore()

    loads = [
        pltpu.make_async_copy(a, b, sem_in.at[i])
        for i, (a, b) in enumerate(
            [
                (rec_hbm.at[0], rec.at[0]), (src_hbm, src_ref), (dead_hbm, dead_ref), (dft_hbm, dft), (lag_hbm, lag),
                (rec_hbm.at[1], rec.at[1]),
            ]
        )
    ]
    for i in (0, 5, 1, 2, 3, 4):
        loads[i].start()

    def greet(k, carry):
        pl.semaphore_signal(barrier, inc=1, device_id={"chan": lax.rem(c + k, chans), "rep": r}, device_id_type=MESH)
        return carry

    lax.fori_loop(1, chans, greet, 0)
    for k in range(1, reps):
        pl.semaphore_signal(barrier, inc=1, device_id={"chan": c, "rep": lax.rem(r + k, reps)}, device_id_type=MESH)

    loads[0].wait()

    def pack_window(w):
        def pack(i, carry):
            for k in range(8):
                g = i * 8 + k
                packed[w, g] = jnp.concatenate([rec[w, g, 0:16], rec[w, g, 16:32]], axis=1)
            return carry

        lax.fori_loop(0, chans // 8, pack, 0)
        recv[w, c] = packed[w, c]

    pack_window(0)
    pl.semaphore_wait(barrier, chans - 1 + reps - 1)

    some_zero = chans * 3 // 8

    def send_part(w, first, last):
        def send(k, carry):
            d = lax.rem(c + k, chans)
            pltpu.make_async_remote_copy(
                packed.at[w, d], recv.at[w, c], a_send.at[w], a_recv.at[w],
                device_id={"chan": d, "rep": r}, device_id_type=MESH,
            ).start()
            return carry

        lax.fori_loop(first, last, send, 0)

    send_part(0, 1, some_zero)
    loads[5].wait()
    pack_window(1)

    loads[1].wait()
    src = src_ref[...]
    within = src & 255
    mine = jnp.where((within >> 6) == r, within & 63, -1000)
    row = iota((128, 128), 0)
    sel = jnp.concatenate([(row == mine).astype(BF16), (row - 64 == mine).astype(BF16)], axis=1)
    block = src >> 8
    block2 = jnp.concatenate([block, block], axis=1)
    accs = []
    for w in range(2):
        cols[...] = jnp.dot(packed[w].reshape(chans * 16, 128), sel, preferred_element_type=F32)

        def pick(i, acc):
            for k in range(8):
                g = i * 8 + k
                part = cols[pl.ds(pl.multiple_of(g * 16, 16), 16), :]
                acc = acc + jnp.where(block2 == g, part, 0.0)
            return acc

        accs.append(lax.fori_loop(0, chans // 8, pick, jnp.zeros((16, 256), F32)))
    lane = iota((16, 128), 1)
    for q in range(reps):
        value = jnp.zeros((16, 128), F32)
        for th in range(2):
            for w in range(2):
                to = th * 64 + w * 32
                piece = pltpu.roll(accs[w][:, th * 128 : th * 128 + 128], (to - 32 * q) % 128, 1)
                value = jnp.where((lane >= to) & (lane < to + 32), piece, value)
        picks[q] = value.astype(BF16)
    pickrecv[r] = picks[r]

    def p_copy(k):
        d = lax.rem(r + k, reps)
        return pltpu.make_async_remote_copy(
            picks.at[d], pickrecv.at[r], p_send.at[k], p_recv.at[k], device_id={"chan": c, "rep": d}, device_id_type=MESH
        )

    for k in range(1, reps):
        p_copy(k).start()
    send_part(0, some_zero, chans)

    loads[2].wait()
    dead = dead_ref[...]
    eye = iota((128, 128), 0) == iota((128, 128), 1)
    src_col = jnp.sum(jnp.where(eye, jnp.broadcast_to(src, (128, 128)), 0), axis=1, keepdims=True)
    ones = jnp.ones((8, 1024), BF16)
    chan_live = []
    for w in range(2):
        listed = dead[w : w + 1, :]
        hit = jnp.sum((listed == src_col).astype(F32), axis=1, keepdims=True)
        livesrc[w] = jnp.broadcast_to(jnp.where(hit > 0.5, 0.0, 1.0), (128, 128))
        here = jnp.where((listed >> 8) == c, listed & 255, -1)
        onehot = (iota((256, 1024), 0) == here).astype(BF16)
        hits = lax.dot_general(ones, onehot, (((1,), (1,)), ((), ())), preferred_element_type=F32)
        chan_live.append(jnp.where(hits[0:1] > 0.5, 0.0, 1.0))
    start = pl.multiple_of(r * 32, 32)
    ls = [livesrc[w, pl.ds(start, 32), :] for w in range(2)]
    for h in range(2):
        span = slice(h * 128, h * 128 + 128)
        pairs = ls[0] * chan_live[0][:, span] + ls[1] * chan_live[1][:, span]
        inv[:, span] = 1.0 / (math.sqrt(K) * jnp.maximum(pairs, 1.0))

    for k in range(1, reps):
        p_copy(k).wait_send()
        p_copy(k).wait_recv()
    total = pickrecv[0].astype(F32)
    for q in range(1, reps):
        total = total + pickrecv[q].astype(F32)
    srcbuf[c] = total.astype(BF16)

    def z_start(k, carry):
        pltpu.make_async_remote_copy(
            srcbuf.at[c], srcbuf.at[c], z_send, z_recv,
            device_id={"chan": yx * Z + lax.rem(z + k, Z), "rep": r}, device_id_type=MESH,
        ).start()
        return carry

    def y_start(k, carry):
        span = srcbuf.at[pl.ds(yx * Z, Z)]
        pltpu.make_async_remote_copy(
            span, span, y_send, y_recv,
            device_id={"chan": lax.rem(yx + k, nyx) * Z + z, "rep": r}, device_id_type=MESH,
        ).start()
        return carry

    sent = []

    def wait_all(some, send, recv):
        bulk = pltpu.make_async_remote_copy(
            some, some, send, recv, device_id={"chan": c, "rep": lax.rem(r + 1, reps)}, device_id_type=MESH
        )
        sent.append(bulk)
        bulk.wait_recv()

    lax.fori_loop(1, Z, z_start, 0)
    send_part(1, 1, chans)
    wait_all(srcbuf.at[pl.ds(0, Z - 1)], z_send, z_recv)
    lax.fori_loop(1, nyx, y_start, 0)
    loads[3].wait()
    loads[4].wait()
    def lag_rows(s, carry):
        at = pl.multiple_of(s * LAGS, LAGS)
        for w in range(2):
            u = srcspec[0, pl.ds(w * 32 + s, 1), :]
            v = srcspec[1, pl.ds(w * 32 + s, 1), :]
            cos, sin = lag[0], lag[1]
            lk = lk1 if w else lk0
            lk[pl.ds(at, LAGS), 0:256] = (u * cos + v * sin).astype(BF16)
            lk[pl.ds(at, LAGS), 256:512] = (v * cos - u * sin).astype(BF16)
        return carry

    def g_copy(w, k):
        return pltpu.make_async_remote_copy(
            gath.at[w, r], gath.at[w, r], g_send.at[w, k], g_recv.at[w, k],
            device_id={"chan": c, "rep": jnp.bitwise_xor(r, k)}, device_id_type=MESH,
        )

    def own_part(w):
        wait_all(recv.at[w, pl.ds(0, chans - 1)], a_send.at[w], a_recv.at[w])
        re, im = whiten(recv.at[w], dft, absbuf, xbuf, normed)
        mask = jnp.zeros((1, 128), F32)
        for q in range(reps):
            tile = chan_live[w][:, (q // 2) * 128 : (q // 2) * 128 + 128]
            mask = jnp.where(r == q, pltpu.roll(tile, (64 * q) % 128, 1), mask)
        re, im = re * mask, im * mask
        gath[w, r] = jnp.where(iota((K, 128), 1) < 64, re, pltpu.roll(im, 64, 1)).astype(BF16)
        for k in (2, 3, 1):
            g_copy(w, k).start()

    def correlate(w):
        for k in range(1, reps):
            g_copy(w, k).wait_recv()
            sent.append(g_copy(w, k))
        low = iota((K, 128), 1) < 64
        to = rhs if w else rhs0
        for h in range(2):
            a, b = gath[w, 2 * h], gath[w, 2 * h + 1]
            to[0:K, h * 128 : h * 128 + 128] = jnp.where(low, a, swap(b))
            to[K:, h * 128 : h * 128 + 128] = jnp.where(low, swap(a), b)
        if w == 0:
            part = jnp.dot(lk0[...], rhs0[...], preferred_element_type=F32)
            for k in range(out.shape[0]):
                out[k] = part[k * LAGS : (k + 1) * LAGS]

    own_part(0)
    own_part(1)
    wait_all(srcbuf.at[pl.ds(0, (nyx - 1) * Z)], y_send, y_recv)
    re, im = whiten(srcbuf, dft, absbuf, xbuf, normed)
    ls_col = jnp.concatenate([ls[0], ls[1]], axis=0)[:, :1]
    for part, value in enumerate((re, im)):
        rows = jnp.transpose(value)[:64] * ls_col
        srcspec[part] = rows.astype(BF16).astype(F32)

    lax.fori_loop(0, 32, lag_rows, 0)

    correlate(0)
    correlate(1)
    for bulk in sent:
        bulk.wait_send()


def correlate_kernel(part, lk, rhs, inv, out, buf, sem):
    parts = sem.shape[0]
    count = out.shape[0] // parts
    copies = []
    for p in range(parts):
        first = p * count
        summed = jnp.dot(lk[first * LAGS : (first + count) * LAGS, :], rhs[...], preferred_element_type=F32)
        for k in range(count):
            buf[first + k] = (part[first + k] + summed[k * LAGS : (k + 1) * LAGS]) * inv[first + k : first + k + 1, :]
        copies.append(pltpu.make_async_copy(buf.at[pl.ds(first, count)], out.at[pl.ds(first, count)], sem.at[p]))
        copies[-1].start()
    for copy in copies:
        copy.wait()


def solution(mesh):
    chans, reps = mesh.shape["chan"], mesh.shape["rep"]

    def shards(records, sources, dead_list):
        windows, groups, width, span = records.shape
        length = span * chans
        dft, lag = tables(length)
        quarter = sources.shape[0] // reps
        vmem = pl.BlockSpec(memory_space=pltpu.VMEM)
        hbm = pl.BlockSpec(memory_space=pltpu.HBM)
        dma = pltpu.SemaphoreType.DMA
        partial = pl.pallas_call(
            functools.partial(gather_kernel, chans, reps),
            out_shape=[
                jax.ShapeDtypeStruct((quarter, LAGS, 256), F32),
                jax.ShapeDtypeStruct((quarter * LAGS, 2 * K), BF16),
                jax.ShapeDtypeStruct((2 * K, 256), BF16),
                jax.ShapeDtypeStruct((quarter, 256), F32),
            ],
            in_specs=[hbm] * 5,
            out_specs=[vmem] * 4,
            scratch_shapes=[
                pltpu.VMEM((windows, groups, span, width), BF16),
                pltpu.VMEM((1, sources.shape[0]), jnp.int32),
                pltpu.VMEM(dead_list.shape, jnp.int32),
                pltpu.VMEM((512, length), BF16),
                pltpu.VMEM((2, LAGS, K), F32),
                pltpu.VMEM((2, chans, 16, 128), BF16),
                pltpu.VMEM((2, chans, 16, 128), BF16),
                pltpu.VMEM((chans * 16, 256), F32),
                pltpu.VMEM((reps, 16, 128), BF16),
                pltpu.VMEM((reps, 16, 128), BF16),
                pltpu.VMEM((chans, 16, 128), BF16),
                pltpu.VMEM((2, reps, K, 128), BF16),
                pltpu.VMEM((2 * K, 256), BF16),
                pltpu.VMEM((quarter * LAGS, 2 * K), BF16),
                pltpu.VMEM((length // 2 + 128, 128), BF16),
                pltpu.VMEM((length // 2, 128), BF16),
                pltpu.VMEM((length // 2, 128), BF16),
                pltpu.VMEM((2, 64, 256), F32),
                pltpu.VMEM((2, 128, 128), F32),
                dma((6,)), dma((2,)), dma((2,)), dma((reps,)), dma((reps,)),
                dma, dma, dma, dma, dma((2, reps)), dma((2, reps)),
            ],
            compiler_params=pltpu.CompilerParams(
                collective_id=0, has_side_effects=True, vmem_limit_bytes=48 << 20
            ),
            name="correlations",
        )(
            *[
                pltpu.with_memory_space_constraint(x, pltpu.HBM)
                for x in (
                    jnp.transpose(records, (0, 1, 3, 2)),
                    sources.reshape(1, -1),
                    dead_list,
                    jnp.asarray(dft),
                    jnp.asarray(lag),
                )
            ]
        )
        return pl.pallas_call(
            correlate_kernel,
            out_shape=jax.ShapeDtypeStruct((quarter, LAGS, 256), F32),
            in_specs=[vmem] * 4,
            out_specs=hbm,
            scratch_shapes=[pltpu.VMEM((quarter, LAGS, 256), F32), dma((4,))],
            compiler_params=pltpu.CompilerParams(vmem_limit_bytes=16 << 20),
            name="correlate",
        )(*partial)

    return jax.shard_map(
        shards,
        mesh=mesh,
        in_specs=(P(None, None, "rep", "chan"), P(), P()),
        out_specs=P("rep", None, "chan"),
        check_vma=False,
    )
```

```python
import functools
import math

import jax
import jax.numpy as jnp
import numpy as np
from jax import lax
from jax.experimental import pallas as pl
from jax.experimental.pallas import tpu as pltpu
from jax.sharding import PartitionSpec as P

K = 256
K0 = 16
HALF = 32
WH = 32
LAGS = 64
EPS = 1e-06
Z = 8

MESH = pl.DeviceIdType.MESH
BF16 = jnp.bfloat16
F32 = jnp.float32


def tables(length):
    m = ((K0 + np.arange(K))[:, None] * np.arange(length)[None, :]) % length
    angle = m.astype(np.float64) * (2.0 * math.pi / length)
    dft = np.concatenate([np.cos(angle), -np.sin(angle)], axis=0).astype(jnp.bfloat16)
    tau = np.arange(LAGS)[:, None] - LAGS // 2
    phi = ((tau * (K0 + np.arange(K))[None, :]) % length).astype(np.float64) * (2.0 * math.pi / length)
    lag = np.stack([np.cos(phi), np.sin(phi)]).astype(np.float32)
    return dft, lag


def iota(shape, axis):
    return lax.broadcasted_iota(jnp.int32, shape, axis)


def swap(x):
    return pltpu.roll(x, 64, 1)


def whiten(buf, dft, absbuf, xbuf, normed):
    blocks = buf.shape[0]
    top = blocks * 16
    low = iota((16, 128), 1) < 64

    def spread(b, carry):
        for i in range(8):
            at = b * 8 + i
            first, second = buf[at], buf[at + blocks // 2]
            x0 = jnp.where(low, first, swap(second))
            x1 = jnp.where(low, swap(first), second)
            rows = pl.multiple_of(at * 32, 32)
            xbuf[pl.ds(rows, 16), :] = x0
            xbuf[pl.ds(rows + 16, 16), :] = x1
            absbuf[pl.ds(rows + 64, 16), :] = jnp.abs(x0)
            absbuf[pl.ds(rows + 80, 16), :] = jnp.abs(x1)
        return carry

    lax.fori_loop(0, blocks // 16, spread, 0)
    low = iota((64, 128), 1) < 64
    zero = jnp.zeros((64, 128), BF16)
    absbuf[0:64, :] = jnp.where(low, zero, swap(absbuf[top : top + 64, :]))
    absbuf[top + 64 :, :] = jnp.where(low, swap(absbuf[64:128, :]), zero)
    band = (jnp.abs(iota((128, 256), 1) - 64 - iota((128, 256), 0)) <= HALF).astype(BF16)

    for b in range(top // 128):
        start = b * 128
        total = jnp.dot(band, absbuf[pl.ds(start, 256), :], preferred_element_type=F32)
        t = iota((128, 128), 0) + b * 128 + jnp.where(iota((128, 128), 1) < 64, 0, top)
        n = (jnp.minimum(t, HALF) + jnp.minimum(2 * top - 1 - t, HALF) + 1).astype(F32)
        x = xbuf[pl.ds(start, 128), :].astype(F32)
        normed[pl.ds(start, 128), :] = (x * n / (total + EPS * n)).astype(BF16)
    x = normed[...]
    spectrum = jnp.dot(dft[:, :top], x, preferred_element_type=F32)
    other = jnp.dot(dft[:, top:], x, preferred_element_type=F32)
    spectrum = spectrum + pltpu.roll(other, 64, 1)
    re, im = spectrum[:K], spectrum[K:]
    amp = jnp.sqrt(re * re + im * im)
    high = amp.astype(BF16)
    rest = amp - high.astype(F32)
    mid = rest.astype(BF16)
    near = (jnp.abs(iota((K, K), 0) - iota((K, K), 1)) <= WH).astype(BF16)
    total = jnp.dot(near, mid, preferred_element_type=F32) + jnp.dot(near, high, preferred_element_type=F32)
    j = iota((K, 128), 0)
    n = (jnp.minimum(j, WH) + jnp.minimum(K - 1 - j, WH) + 1).astype(F32)
    scale = 1.0 / (total / n + EPS)
    return re * scale, im * scale


def gather_kernel(
    chans, reps,
    rec_hbm, src_hbm, dead_hbm, dft_hbm, lag_hbm,
    out, lk1, rhs, inv,
    rec, src_ref, dead_ref, dft, lag,
    packed, recv, cols, picks, pickrecv, srcbuf, gath, rhs0, lk0, absbuf, xbuf, normed, srcspec, livesrc,
    sem_in, a_send, a_recv, p_send, p_recv, z_send, z_recv, y_send, y_recv, g_send, g_recv,
):
    c, r = lax.axis_index("chan"), lax.axis_index("rep")
    z, yx = lax.rem(c, Z), c // Z
    nyx = chans // Z
    barrier = pltpu.get_barrier_semaphore()

    loads = [
        pltpu.make_async_copy(a, b, sem_in.at[i])
        for i, (a, b) in enumerate(
            [
                (rec_hbm.at[0], rec.at[0]), (src_hbm, src_ref), (dead_hbm, dead_ref), (dft_hbm, dft), (lag_hbm, lag),
                (rec_hbm.at[1], rec.at[1]),
            ]
        )
    ]
    for i in (0, 5, 1, 2, 3, 4):
        loads[i].start()

    def greet(k, carry):
        pl.semaphore_signal(barrier, inc=1, device_id={"chan": lax.rem(c + k, chans), "rep": r}, device_id_type=MESH)
        return carry

    lax.fori_loop(1, chans, greet, 0)
    for k in range(1, reps):
        pl.semaphore_signal(barrier, inc=1, device_id={"chan": c, "rep": lax.rem(r + k, reps)}, device_id_type=MESH)

    loads[0].wait()

    def pack_window(w):
        def pack(i, carry):
            for k in range(8):
                g = i * 8 + k
                packed[w, g] = jnp.concatenate([rec[w, g, 0:16], rec[w, g, 16:32]], axis=1)
            return carry

        lax.fori_loop(0, chans // 8, pack, 0)
        recv[w, c] = packed[w, c]

    pack_window(0)
    pl.semaphore_wait(barrier, chans - 1 + reps - 1)

    some_zero = chans * 3 // 8

    def send_part(w, first, last):
        def send(k, carry):
            d = lax.rem(c + k, chans)
            pltpu.make_async_remote_copy(
                packed.at[w, d], recv.at[w, c], a_send.at[w], a_recv.at[w],
                device_id={"chan": d, "rep": r}, device_id_type=MESH,
            ).start()
            return carry

        lax.fori_loop(first, last, send, 0)

    send_part(0, 1, some_zero)
    loads[5].wait()
    pack_window(1)

    loads[1].wait()
    src = src_ref[...]
    within = src & 255
    mine = jnp.where((within >> 6) == r, within & 63, -1000)
    row = iota((128, 128), 0)
    sel = jnp.concatenate([(row == mine).astype(BF16), (row - 64 == mine).astype(BF16)], axis=1)
    block = src >> 8
    block2 = jnp.concatenate([block, block], axis=1)
    accs = []
    for w in range(2):
        cols[...] = jnp.dot(packed[w].reshape(chans * 16, 128), sel, preferred_element_type=F32)

        def pick(i, acc):
            for k in range(8):
                g = i * 8 + k
                part = cols[pl.ds(pl.multiple_of(g * 16, 16), 16), :]
                acc = acc + jnp.where(block2 == g, part, 0.0)
            return acc

        accs.append(lax.fori_loop(0, chans // 8, pick, jnp.zeros((16, 256), F32)))
    lane = iota((16, 128), 1)
    for q in range(reps):
        value = jnp.zeros((16, 128), F32)
        for th in range(2):
            for w in range(2):
                to = th * 64 + w * 32
                piece = pltpu.roll(accs[w][:, th * 128 : th * 128 + 128], (to - 32 * q) % 128, 1)
                value = jnp.where((lane >= to) & (lane < to + 32), piece, value)
        picks[q] = value.astype(BF16)
    pickrecv[r] = picks[r]

    def p_copy(k):
        d = lax.rem(r + k, reps)
        return pltpu.make_async_remote_copy(
            picks.at[d], pickrecv.at[r], p_send.at[k], p_recv.at[k], device_id={"chan": c, "rep": d}, device_id_type=MESH
        )

    for k in range(1, reps):
        p_copy(k).start()
    send_part(0, some_zero, chans)

    send_part(1, 1, chans)

    loads[2].wait()
    dead = dead_ref[...]
    eye = iota((128, 128), 0) == iota((128, 128), 1)
    src_col = jnp.sum(jnp.where(eye, jnp.broadcast_to(src, (128, 128)), 0), axis=1, keepdims=True)
    ones = jnp.ones((8, 1024), BF16)
    chan_live = []
    for w in range(2):
        listed = dead[w : w + 1, :]
        hit = jnp.sum((listed == src_col).astype(F32), axis=1, keepdims=True)
        livesrc[w] = jnp.broadcast_to(jnp.where(hit > 0.5, 0.0, 1.0), (128, 128))
        here = jnp.where((listed >> 8) == c, listed & 255, -1)
        onehot = (iota((256, 1024), 0) == here).astype(BF16)
        hits = lax.dot_general(ones, onehot, (((1,), (1,)), ((), ())), preferred_element_type=F32)
        chan_live.append(jnp.where(hits[0:1] > 0.5, 0.0, 1.0))
    start = pl.multiple_of(r * 32, 32)
    ls = [livesrc[w, pl.ds(start, 32), :] for w in range(2)]
    for h in range(2):
        span = slice(h * 128, h * 128 + 128)
        pairs = ls[0] * chan_live[0][:, span] + ls[1] * chan_live[1][:, span]
        inv[:, span] = 1.0 / (math.sqrt(K) * jnp.maximum(pairs, 1.0))

    for k in range(1, reps):
        p_copy(k).wait_send()
        p_copy(k).wait_recv()
    total = pickrecv[0].astype(F32)
    for q in range(1, reps):
        total = total + pickrecv[q].astype(F32)
    srcbuf[c] = total.astype(BF16)

    def z_start(k, carry):
        pltpu.make_async_remote_copy(
            srcbuf.at[c], srcbuf.at[c], z_send, z_recv,
            device_id={"chan": yx * Z + lax.rem(z + k, Z), "rep": r}, device_id_type=MESH,
        ).start()
        return carry

    def y_start(k, carry):
        span = srcbuf.at[pl.ds(yx * Z, Z)]
        pltpu.make_async_remote_copy(
            span, span, y_send, y_recv,
            device_id={"chan": lax.rem(yx + k, nyx) * Z + z, "rep": r}, device_id_type=MESH,
        ).start()
        return carry

    sent = []

    def wait_all(some, send, recv):
        bulk = pltpu.make_async_remote_copy(
            some, some, send, recv, device_id={"chan": c, "rep": lax.rem(r + 1, reps)}, device_id_type=MESH
        )
        sent.append(bulk)
        bulk.wait_recv()

    lax.fori_loop(1, Z, z_start, 0)
    wait_all(srcbuf.at[pl.ds(0, Z - 1)], z_send, z_recv)
    lax.fori_loop(1, nyx, y_start, 0)
    loads[3].wait()
    loads[4].wait()
    def lag_rows(s, carry):
        at = pl.multiple_of(s * LAGS, LAGS)
        for w in range(2):
            u = srcspec[0, pl.ds(w * 32 + s, 1), :]
            v = srcspec[1, pl.ds(w * 32 + s, 1), :]
            cos, sin = lag[0], lag[1]
            lk = lk1 if w else lk0
            lk[pl.ds(at, LAGS), 0:256] = (u * cos + v * sin).astype(BF16)
            lk[pl.ds(at, LAGS), 256:512] = (v * cos - u * sin).astype(BF16)
        return carry

    def g_copy(w, k):
        return pltpu.make_async_remote_copy(
            gath.at[w, r], gath.at[w, r], g_send.at[w, k], g_recv.at[w, k],
            device_id={"chan": c, "rep": jnp.bitwise_xor(r, k)}, device_id_type=MESH,
        )

    def own_part(w):
        wait_all(recv.at[w, pl.ds(0, chans - 1)], a_send.at[w], a_recv.at[w])
        re, im = whiten(recv.at[w], dft, absbuf, xbuf, normed)
        mask = jnp.zeros((1, 128), F32)
        for q in range(reps):
            tile = chan_live[w][:, (q // 2) * 128 : (q // 2) * 128 + 128]
            mask = jnp.where(r == q, pltpu.roll(tile, (64 * q) % 128, 1), mask)
        re, im = re * mask, im * mask
        gath[w, r] = jnp.where(iota((K, 128), 1) < 64, re, pltpu.roll(im, 64, 1)).astype(BF16)
        for k in (2, 3, 1):
            g_copy(w, k).start()

    def correlate(w):
        for k in range(1, reps):
            g_copy(w, k).wait_recv()
            sent.append(g_copy(w, k))
        low = iota((K, 128), 1) < 64
        to = rhs if w else rhs0
        for h in range(2):
            a, b = gath[w, 2 * h], gath[w, 2 * h + 1]
            to[0:K, h * 128 : h * 128 + 128] = jnp.where(low, a, swap(b))
            to[K:, h * 128 : h * 128 + 128] = jnp.where(low, swap(a), b)
        if w == 0:
            part = jnp.dot(lk0[...], rhs0[...], preferred_element_type=F32)
            for k in range(out.shape[0]):
                out[k] = part[k * LAGS : (k + 1) * LAGS]

    own_part(0)
    own_part(1)
    wait_all(srcbuf.at[pl.ds(0, (nyx - 1) * Z)], y_send, y_recv)
    re, im = whiten(srcbuf, dft, absbuf, xbuf, normed)
    ls_col = jnp.concatenate([ls[0], ls[1]], axis=0)[:, :1]
    for part, value in enumerate((re, im)):
        rows = jnp.transpose(value)[:64] * ls_col
        srcspec[part] = rows.astype(BF16).astype(F32)

    lax.fori_loop(0, 32, lag_rows, 0)

    correlate(0)
    correlate(1)
    for bulk in sent:
        bulk.wait_send()


def correlate_kernel(part, lk, rhs, inv, out, buf, sem):
    parts = sem.shape[0]
    count = out.shape[0] // parts
    copies = []
    for p in range(parts):
        first = p * count
        summed = jnp.dot(lk[first * LAGS : (first + count) * LAGS, :], rhs[...], preferred_element_type=F32)
        for k in range(count):
            buf[first + k] = (part[first + k] + summed[k * LAGS : (k + 1) * LAGS]) * inv[first + k : first + k + 1, :]
        copies.append(pltpu.make_async_copy(buf.at[pl.ds(first, count)], out.at[pl.ds(first, count)], sem.at[p]))
        copies[-1].start()
    for copy in copies:
        copy.wait()


def solution(mesh):
    chans, reps = mesh.shape["chan"], mesh.shape["rep"]

    def shards(records, sources, dead_list):
        windows, groups, width, span = records.shape
        length = span * chans
        dft, lag = tables(length)
        quarter = sources.shape[0] // reps
        vmem = pl.BlockSpec(memory_space=pltpu.VMEM)
        hbm = pl.BlockSpec(memory_space=pltpu.HBM)
        dma = pltpu.SemaphoreType.DMA
        partial = pl.pallas_call(
            functools.partial(gather_kernel, chans, reps),
            out_shape=[
                jax.ShapeDtypeStruct((quarter, LAGS, 256), F32),
                jax.ShapeDtypeStruct((quarter * LAGS, 2 * K), BF16),
                jax.ShapeDtypeStruct((2 * K, 256), BF16),
                jax.ShapeDtypeStruct((quarter, 256), F32),
            ],
            in_specs=[hbm] * 5,
            out_specs=[vmem] * 4,
            scratch_shapes=[
                pltpu.VMEM((windows, groups, span, width), BF16),
                pltpu.VMEM((1, sources.shape[0]), jnp.int32),
                pltpu.VMEM(dead_list.shape, jnp.int32),
                pltpu.VMEM((512, length), BF16),
                pltpu.VMEM((2, LAGS, K), F32),
                pltpu.VMEM((2, chans, 16, 128), BF16),
                pltpu.VMEM((2, chans, 16, 128), BF16),
                pltpu.VMEM((chans * 16, 256), F32),
                pltpu.VMEM((reps, 16, 128), BF16),
                pltpu.VMEM((reps, 16, 128), BF16),
                pltpu.VMEM((chans, 16, 128), BF16),
                pltpu.VMEM((2, reps, K, 128), BF16),
                pltpu.VMEM((2 * K, 256), BF16),
                pltpu.VMEM((quarter * LAGS, 2 * K), BF16),
                pltpu.VMEM((length // 2 + 128, 128), BF16),
                pltpu.VMEM((length // 2, 128), BF16),
                pltpu.VMEM((length // 2, 128), BF16),
                pltpu.VMEM((2, 64, 256), F32),
                pltpu.VMEM((2, 128, 128), F32),
                dma((6,)), dma((2,)), dma((2,)), dma((reps,)), dma((reps,)),
                dma, dma, dma, dma, dma((2, reps)), dma((2, reps)),
            ],
            compiler_params=pltpu.CompilerParams(
                collective_id=0, has_side_effects=True, vmem_limit_bytes=48 << 20
            ),
            name="correlations",
        )(
            *[
                pltpu.with_memory_space_constraint(x, pltpu.HBM)
                for x in (
                    jnp.transpose(records, (0, 1, 3, 2)),
                    sources.reshape(1, -1),
                    dead_list,
                    jnp.asarray(dft),
                    jnp.asarray(lag),
                )
            ]
        )
        return pl.pallas_call(
            correlate_kernel,
            out_shape=jax.ShapeDtypeStruct((quarter, LAGS, 256), F32),
            in_specs=[vmem] * 4,
            out_specs=hbm,
            scratch_shapes=[pltpu.VMEM((quarter, LAGS, 256), F32), dma((4,))],
            compiler_params=pltpu.CompilerParams(vmem_limit_bytes=16 << 20),
            name="correlate",
        )(*partial)

    return jax.shard_map(
        shards,
        mesh=mesh,
        in_specs=(P(None, None, "rep", "chan"), P(), P()),
        out_specs=P("rep", None, "chan"),
        check_vma=False,
    )
```
